128 devices in a mesh: ctx: 4 (over x), ch: 32 (over z, y, core).
Axes of the slice: x: 4, y: 4, z: 4, core: 2. Of those that a mesh axis runs over, the one named last changes fastest.
Arguments:
- features: bfloat16 [3, 512, 8192], P(None, 'ctx', 'ch'), may hold values from -6 to 6
- short_kernel: float32 [3, 7, 8192], P(None, None, 'ch'), may hold values from -2 to 2
- long_filter: bfloat16 [512, 8192], P('ctx', 'ch'), may hold values from -0.25 to 0.25
- out_weight: bfloat16 [8192, 8192], P(None, 'ch'), may hold values from -0.0625 to 0.0625
- grad_out: bfloat16 [512, 8192], P('ctx', 'ch'), may hold values from -6 to 6
Outputs:
- grad_features: bfloat16 [3, 512, 8192], P(None, 'ctx', 'ch')
- grad_kernel: float32 [3, 7, 8192], P(None, None, 'ch')
- grad_filter: float32 [512, 8192], P('ctx', 'ch')
- grad_weight: float32 [8192, 8192], P('ctx', 'ch')
The draws below stay inside these ranges and needn't reach their ends.
All inputs are finite; a program needn't handle non-finite values.
Results may differ from the reference program's by a relative error of at most 0.0051.
Values may be sent and summed in bfloat16 or wider, within the bound.
No kernel may reach another device: no remote copies, remote signals or barrier semaphores. Data moves between devices by JAX's collectives and lax.ppermute only.
A program may use at most 64 MiB of HBM per device.

```python
import jax
import jax.numpy as jnp
from jax import lax

D = 8192
SHORT = 7
LENGTH = 512


def block_scale(rng, extent, pieces, least, high):
    factor_of, own = 1.0, jax.random.fold_in(rng, 6)
    for position, shards_of in pieces:
        heights = jnp.exp(jax.random.uniform(jax.random.fold_in(own, position), (shards_of,), jnp.float32, least / len(pieces), high / len(pieces)))
        factor_of = factor_of * jnp.repeat(heights, extent[position] // shards_of).reshape([-1 if axis == position else 1 for axis in range(len(extent))])
    return factor_of


def scatter_about(key, extent, spread, most, pieces=(), held_as=jnp.bfloat16):
    level = block_scale(key, extent, pieces, -0.22, 0.18) if pieces else 1.0
    entries = jax.random.normal(key, extent, jnp.float32) * spread * level
    return jnp.minimum(jnp.maximum(entries, -most), most).astype(held_as)


def setup_inputs(seed: int = 0) -> dict:
    keys = jax.random.split(jax.random.key(seed), 6)
    return {
        "features": scatter_about(keys[0], (3, LENGTH, D), 1.0, 6.0, ((1, 4), (2, 32))),
        "short_kernel": scatter_about(keys[1], (3, SHORT, D), SHORT ** -0.5, 2.0, ((2, 32),), jnp.float32),
        "long_filter": scatter_about(keys[2], (LENGTH, D), LENGTH ** -0.5, 0.25, ((0, 4), (1, 32))),
        "out_weight": scatter_about(keys[3], (D, D), D ** -0.5, 0.0625, ((1, 32),)),
        "grad_out": scatter_about(keys[4], (LENGTH, D), 1.0, 6.0, ((0, 4), (1, 32))),
    }


def shift_down(values, steps):
    return jnp.pad(values, ((steps, 0), (0, 0)))[:values.shape[0]]


def shift_up(values, steps):
    return jnp.pad(values, ((0, steps), (0, 0)))[steps:]


def reference(features, short_kernel, long_filter, out_weight, grad_out):
    feats = features.astype(jnp.float32)
    length = feats.shape[1]
    convs = []
    for branch in range(3):
        total = jnp.zeros_like(feats[branch])
        for tap_index in range(SHORT):
            total = total + short_kernel[branch, tap_index] * shift_down(feats[branch], tap_index)
        convs.append(total)
    q_conv, k_conv, v_conv = convs
    gated = (k_conv * v_conv).astype(jnp.bfloat16)
    gated_wide = lax.optimization_barrier(gated).astype(jnp.float32)
    period = 2 * length
    filter_spec = jnp.fft.rfft(long_filter.astype(jnp.float32), n=period, axis=0)
    gated_spec = jnp.fft.rfft(gated_wide, n=period, axis=0)
    long_out = jnp.fft.irfft(filter_spec * gated_spec, n=period, axis=0)[:length]
    mixed = (q_conv * long_out).astype(jnp.bfloat16)
    grad_mixed = jnp.dot(grad_out, out_weight.T, preferred_element_type=jnp.float32)
    grad_long = (grad_mixed * q_conv).astype(jnp.bfloat16)
    grad_long_wide = lax.optimization_barrier(grad_long).astype(jnp.float32)
    grad_spec = jnp.fft.rfft(grad_long_wide, n=period, axis=0)
    grad_gated = jnp.fft.irfft(jnp.conj(filter_spec) * grad_spec, n=period, axis=0)[:length]
    grad_filter = jnp.fft.irfft(jnp.conj(gated_spec) * grad_spec, n=period, axis=0)[:length]
    grad_conv = [grad_mixed * long_out, grad_gated * v_conv, grad_gated * k_conv]
    feature_grads = []
    kernel_grads = []
    for branch in range(3):
        total = jnp.zeros_like(feats[branch])
        rows = []
        for tap_index in range(SHORT):
            total = total + short_kernel[branch, tap_index] * shift_up(grad_conv[branch], tap_index)
            rows.append(jnp.sum(grad_conv[branch] * shift_down(feats[branch], tap_index), axis=0))
        feature_grads.append(total.astype(jnp.bfloat16))
        kernel_grads.append(jnp.stack(rows, axis=0))
    grad_features = jnp.stack(feature_grads, axis=0)
    grad_kernel = jnp.stack(kernel_grads, axis=0)
    grad_weight = jnp.dot(mixed.T, grad_out, preferred_element_type=jnp.float32)
    return grad_features, grad_kernel, grad_filter, grad_weight
```

```python
import functools
import math

import jax
import jax.numpy as jnp
import numpy as np
from jax import lax
from jax.experimental import pallas as pl
from jax.experimental.pallas import tpu as pltpu
from jax.sharding import PartitionSpec as P

F32 = jnp.float32
BF16 = jnp.bfloat16
NX, NZ, NY, NC = 4, 4, 4, 2
TAPS = 7
NT = (((1,), (1,)), ((), ()))
VMEM_LIMIT = 56 * 1024 * 1024


def coords():
    x = lax.axis_index("ctx")
    ch = lax.axis_index("ch")
    return x, ch // 8, lax.rem(ch // 2, 4), lax.rem(ch, 2)


def flat(x, z, y, c):
    return ((x * NZ + z) * NY + y) * NC + c


def move(array, rule):
    pairs = []
    for x in range(NX):
        for z in range(NZ):
            for y in range(NY):
                for c in range(NC):
                    pairs.append((flat(x, z, y, c), flat(*rule(x, z, y, c))))
    return lax.ppermute(array, ("ctx", "ch"), pairs)


def along_x(array, by):
    return move(array, lambda x, z, y, c: ((x + by) % NX, z, y, c))


def along_z(array, by):
    return move(array, lambda x, z, y, c: (x, (z + by) % NZ, y, c))


def along_y(array, by):
    return move(array, lambda x, z, y, c: (x, z, (y + by) % NY, c))


def other_core(array):
    return move(array, lambda x, z, y, c: (x, z, y, 1 - c))


def turned(array, by):
    return move(array, lambda x, z, y, c: (z, (x + by) % NZ, y, c))


def wave_table(length):
    period = 2 * length
    freq = 2 * np.arange(length) + 1
    steps = np.arange(length)
    angle = (steps[:, None] * freq[None, :] % (2 * period)) * (math.pi / period)
    table = np.concatenate([np.cos(angle), -np.sin(angle)], axis=1)
    high = table.astype(jnp.bfloat16)
    low = (table - high.astype(np.float64)).astype(jnp.bfloat16)
    return high, low


def call(kernel, out_shape, *args, scratch=(), in_specs=None):
    return pl.pallas_call(
        kernel,
        out_shape=out_shape,
        in_specs=in_specs or [pl.BlockSpec(memory_space=pltpu.VMEM)] * len(args),
        out_specs=jax.tree.map(lambda _: pl.BlockSpec(memory_space=pltpu.VMEM), out_shape),
        scratch_shapes=list(scratch),
        compiler_params=pltpu.CompilerParams(vmem_limit_bytes=VMEM_LIMIT),
    )(*args)


def shape(dims, dtype):
    return jax.ShapeDtypeStruct(dims, dtype)


def pack_kernel(feat_ref, filt_ref, taps_ref, p0, p1, p2, p3, taps_out, held, taps_held):
    x = coords()[0]
    for stream in range(4):
        block = feat_ref[stream] if stream < 3 else filt_ref[...]
        flipped = block.T
        for quarter in range(4):
            held[quarter, stream] = flipped[quarter * 64 : quarter * 64 + 64]
    for by, out in enumerate((p0, p1, p2, p3)):
        out[...] = held[lax.rem(x + by, 4)]
    rows = jnp.zeros((128, 256), F32)
    taps_held[0] = rows
    for stream in range(3):
        taps_held[0, stream * 8 : stream * 8 + TAPS, :] = taps_ref[stream]
    columns = taps_held[0].T
    for quarter in range(4):
        taps_held[1 + quarter, 0:64, 0:128] = columns[quarter * 64 : quarter * 64 + 64]
    taps_out[...] = taps_held[1 + x, 0:64, 0:128]


def lift_kernel(g0, g1, g2, g3, weight, whole_out, send_out, gathered, rows, sem):
    x, z, y, c = coords()
    copy = pltpu.make_async_copy(weight.at[:, :, 1 - c, x], rows, sem)
    copy.start()
    for by, block in enumerate((g0, g1, g2, g3)):
        gathered[lax.rem(x + 4 - by, 4)] = block[...]
    whole = gathered[...].reshape(512, 256)
    whole_out[...] = whole
    copy.wait()
    for zd in range(NZ):
        part = lax.dot_general(
            rows[zd].reshape(256, 256), whole, NT, preferred_element_type=F32
        )
        send_out[zd] = part.astype(BF16).reshape(NY, 64, 512)


def sum_core_kernel(recv, whole, weight, own_out, s1, s2, s3, rows, sem):
    x, z, y, c = coords()
    copy = pltpu.make_async_copy(weight.at[:, :, c, x], rows, sem)
    copy.start()
    copy.wait()
    for by, out in enumerate((own_out, s1, s2, s3)):
        zd = lax.rem(z + by, 4)
        part = lax.dot_general(
            rows[zd].reshape(256, 256), whole[...], NT, preferred_element_type=F32
        )
        total = part.reshape(NY, 64, 512) + recv[zd].astype(F32)
        out[...] = total.astype(out.dtype)


def sum_z_kernel(own, r1, r2, r3, own_out, s1, s2, s3):
    y = coords()[2]
    for by, out in enumerate((own_out, s1, s2, s3)):
        yd = lax.rem(y + by, 4)
        total = (
            own[yd] + r1[yd].astype(F32) + (r2[yd].astype(F32) + r3[yd].astype(F32))
        )
        out[...] = total.astype(out.dtype)


def later(values, by, lane):
    if by == 0:
        return values
    return jnp.where(lane >= by, pltpu.roll(values, by, 1), 0.0)


def sooner(values, by, lane):
    if by == 0:
        return values
    return jnp.where(lane < 512 - by, pltpu.roll(values, 512 - by, 1), 0.0)


def split(values):
    high = values.astype(BF16)
    return high, (values - high.astype(F32)).astype(BF16)


def forward(rows, high, low):
    return jnp.dot(rows, high[...], preferred_element_type=F32) + jnp.dot(
        rows, low[...], preferred_element_type=F32
    )


def backward(spectra, high, low):
    count = spectra.shape[0]
    big, small = split(spectra)
    first = lax.dot_general(
        jnp.concatenate([big, small], axis=0), high[...], NT, preferred_element_type=F32
    )
    second = lax.dot_general(big, low[...], NT, preferred_element_type=F32)
    return (first[:count] + first[count:] + second) * (1.0 / 512)


def pre_kernel(p0, r1, r2, r3, taps, high, low, mixed_out, conv_out, long_out, spec_out, feat_out, held):
    x = coords()[0]
    for by, block in enumerate((p0, r1, r2, r3)):
        held[lax.rem(x + 4 - by, 4)] = block[...]
    lane = lax.broadcasted_iota(jnp.int32, (64, 512), 1)
    convs = []
    for stream in range(3):
        feats = jnp.concatenate([held[b, stream] for b in range(4)], axis=1)
        feat_out[stream] = feats
        wide = feats.astype(F32)
        total = taps[:, stream * 8 : stream * 8 + 1] * wide
        for tap in range(1, TAPS):
            column = stream * 8 + tap
            total = total + taps[:, column : column + 1] * later(wide, tap, lane)
        conv_out[stream] = total
        convs.append(total)
    gated = (convs[1] * convs[2]).astype(BF16)
    filt = jnp.concatenate([held[b, 3] for b in range(4)], axis=1)
    spec = forward(jnp.concatenate([gated, filt], axis=0), high, low)
    spec_out[...] = spec
    gr, gi = spec[:64, :512], spec[:64, 512:]
    hr, hi = spec[64:, :512], spec[64:, 512:]
    product = jnp.concatenate([gr * hr - gi * hi, gr * hi + gi * hr], axis=1)
    long = backward(product, high, low)
    long_out[...] = long
    mixed_out[...] = (convs[0] * long).astype(BF16)


def post_kernel(own, r1, r2, r3, conv, long, spec, feats, taps, high, low, o0, o1, o2, o3, held):
    x = coords()[0]
    lane = lax.broadcasted_iota(jnp.int32, (64, 512), 1)
    grad_mixed = own[...] + r1[...].astype(F32) + (r2[...].astype(F32) + r3[...].astype(F32))
    grad_long = (grad_mixed * conv[0]).astype(BF16)
    lspec = forward(grad_long, high, low)
    lr, li = lspec[:, :512], lspec[:, 512:]
    gr, gi = spec[:64, :512], spec[:64, 512:]
    hr, hi = spec[64:, :512], spec[64:, 512:]
    to_gated = jnp.concatenate([hr * lr + hi * li, hr * li - hi * lr], axis=1)
    to_filter = jnp.concatenate([gr * lr + gi * li, gr * li - gi * lr], axis=1)
    both = backward(jnp.concatenate([to_gated, to_filter], axis=0), high, low)
    grad_gated, grad_filter = both[:64], both[64:]
    grad_conv = (grad_mixed * long[...], grad_gated * conv[2], grad_gated * conv[1])
    slot = lax.broadcasted_iota(jnp.int32, (64, 128), 1)
    sums = jnp.zeros((64, 128), F32)
    for stream in range(3):
        wide = feats[stream].astype(F32)
        total = None
        for tap in range(TAPS):
            column = stream * 8 + tap
            term = taps[:, column : column + 1] * sooner(grad_conv[stream], tap, lane)
            total = term if total is None else total + term
            row = jnp.sum(grad_conv[stream] * later(wide, tap, lane), axis=1, keepdims=True)
            sums = jnp.where(slot == column, row, sums)
        rounded = total.astype(BF16)
        for b in range(4):
            held[b, stream] = rounded[:, b * 128 : b * 128 + 128]
    high_part, low_part = split(grad_filter)
    sums_high, sums_low = split(sums)
    sums_both = sums_high.astype(F32) + pltpu.roll(sums_low.astype(F32), 32, 1)
    for b in range(4):
        held[b, 3] = high_part[:, b * 128 : b * 128 + 128]
        held[b, 4] = low_part[:, b * 128 : b * 128 + 128]
        held[b, 5] = sums_both.astype(BF16)
    for by, out in enumerate((o0, o1, o2, o3)):
        out[...] = held[lax.rem(x + by, 4)]


def out_kernel(o0, r1, r2, r3, feat_out, taps_out, filt_out, held):
    x = coords()[0]
    for by, block in enumerate((o0, r1, r2, r3)):
        held[lax.rem(x + 4 - by, 4)] = block[...]
    for stream in range(3):
        columns = jnp.concatenate([held[q, stream] for q in range(4)], axis=0)
        feat_out[stream] = columns.T
    filt = jnp.concatenate(
        [held[q, 3].astype(F32) + held[q, 4].astype(F32) for q in range(4)], axis=0
    )
    filt_out[...] = filt.T
    sums = jnp.concatenate([held[q, 5].astype(F32) for q in range(4)], axis=0)
    sums = sums + pltpu.roll(sums, 96, 1)
    rows = sums.T
    for stream in range(3):
        taps_out[stream] = rows[stream * 8 : stream * 8 + TAPS]


def weight_kernel(mine, theirs, whole, out):
    x, z, y, c = coords()
    for half, block in enumerate((mine, theirs)):
        core = c if half == 0 else 1 - c
        for back in range(4):
            for along in range(4):
                src = lax.rem(z + 4 - back, 4)
                yd = lax.rem(y + 4 - along, 4)
                part = jnp.dot(block[back, along], whole[...], preferred_element_type=F32)
                start = pl.multiple_of(yd * 512 + core * 256 + src * 64, 64)
                out[pl.ds(start, 64), :] = part


def local(high, low, features, short_kernel, long_filter, out_weight, grad_out):
    high, low = jnp.asarray(high), jnp.asarray(low)
    weight = out_weight.reshape(NZ, NY, NC, NX, 64, 256)
    piece = shape((4, 64, 128), BF16)
    g = [grad_out] + [along_x(grad_out, k) for k in (1, 2, 3)]
    *pay, taps = call(
        pack_kernel,
        [piece] * 4 + [shape((64, 128), F32)],
        features,
        long_filter,
        short_kernel,
        scratch=[pltpu.VMEM((4, 4, 64, 128), BF16), pltpu.VMEM((5, 128, 256), F32)],
    )
    got = [pay[0]] + [along_x(pay[k], k) for k in (1, 2, 3)]
    vmem = pl.BlockSpec(memory_space=pltpu.VMEM)
    hbm = pl.BlockSpec(memory_space=pl.ANY)
    whole, send = call(
        lift_kernel,
        [shape((512, 256), BF16), shape((NZ, NY, 64, 512), BF16)],
        *g,
        weight,
        in_specs=[vmem] * 4 + [hbm],
        scratch=[
            pltpu.VMEM((4, 128, 256), BF16),
            pltpu.VMEM((NZ, NY, 64, 256), BF16),
            pltpu.SemaphoreType.DMA,
        ],
    )
    recv = other_core(send)
    own, *sends = call(
        sum_core_kernel,
        [shape((NY, 64, 512), F32)] + [shape((NY, 64, 512), BF16)] * 3,
        recv,
        whole,
        weight,
        in_specs=[vmem, vmem, hbm],
        scratch=[pltpu.VMEM((NZ, NY, 64, 256), BF16), pltpu.SemaphoreType.DMA],
    )
    recvs = [along_z(sends[k - 1], k) for k in (1, 2, 3)]
    mixed, conv, long, spec, feats = call(
        pre_kernel,
        [
            shape((64, 512), BF16),
            shape((3, 64, 512), F32),
            shape((64, 512), F32),
            shape((128, 1024), F32),
            shape((3, 64, 512), BF16),
        ],
        *got,
        taps,
        high,
        low,
        scratch=[pltpu.VMEM((4, 4, 64, 128), BF16)],
    )
    mixed_y = jnp.stack([mixed] + [along_y(mixed, k) for k in (1, 2, 3)])
    own, *sends = call(
        sum_z_kernel,
        [shape((64, 512), F32)] + [shape((64, 512), BF16)] * 3,
        own,
        *recvs,
    )
    recvs = [along_y(sends[k - 1], k) for k in (1, 2, 3)]
    mine = jnp.stack([turned(mixed_y, k) for k in range(4)])
    theirs = other_core(mine)
    piece = shape((6, 64, 128), BF16)
    outs = call(
        post_kernel,
        [piece] * 4,
        own,
        *recvs,
        conv,
        long,
        spec,
        feats,
        taps,
        high,
        low,
        scratch=[pltpu.VMEM((4, 6, 64, 128), BF16)],
    )
    backs = [outs[0]] + [along_x(outs[k], k) for k in (1, 2, 3)]
    grad_features, grad_kernel, grad_filter = call(
        out_kernel,
        [shape((3, 128, 256), BF16), shape((3, TAPS, 256), F32), shape((128, 256), F32)],
        *backs,
        scratch=[pltpu.VMEM((4, 6, 64, 128), BF16)],
    )
    grad_weight = call(weight_kernel, shape((2048, 256), F32), mine, theirs, whole)
    return grad_features, grad_kernel, grad_filter, grad_weight


def solution(mesh):
    high, low = wave_table(512)
    return jax.shard_map(
        functools.partial(local, high, low),
        mesh=mesh,
        in_specs=(
            P(None, "ctx", "ch"),
            P(None, None, "ch"),
            P("ctx", "ch"),
            P(None, "ch"),
            P("ctx", "ch"),
        ),
        out_specs=(P(None, "ctx", "ch"), P(None, None, "ch"), P("ctx", "ch"), P("ctx", "ch")),
        check_vma=False,
    )
```

```python
import functools
import math

import jax
import jax.numpy as jnp
import numpy as np
from jax import lax
from jax.experimental import pallas as pl
from jax.experimental.pallas import tpu as pltpu
from jax.sharding import PartitionSpec as P

F32 = jnp.float32
BF16 = jnp.bfloat16
NX, NZ, NY, NC = 4, 4, 4, 2
TAPS = 7
NT = (((1,), (1,)), ((), ()))
VMEM_LIMIT = 20 * 1024 * 1024
WEIGHT = 3.5e10


def coords():
    x = lax.axis_index("ctx")
    ch = lax.axis_index("ch")
    return x, ch // 8, lax.rem(ch // 2, 4), lax.rem(ch, 2)


def flat(x, z, y, c):
    return ((x * NZ + z) * NY + y) * NC + c


def move(array, rule):
    pairs = []
    for x in range(NX):
        for z in range(NZ):
            for y in range(NY):
                for c in range(NC):
                    pairs.append((flat(x, z, y, c), flat(*rule(x, z, y, c))))
    return lax.ppermute(array, ("ctx", "ch"), pairs)


def along_x(array, by):
    return move(array, lambda x, z, y, c: ((x + by) % NX, z, y, c))


def along_z(array, by):
    return move(array, lambda x, z, y, c: (x, (z + by) % NZ, y, c))


def along_y(array, by):
    return move(array, lambda x, z, y, c: (x, z, (y + by) % NY, c))


def other_core(array):
    return move(array, lambda x, z, y, c: (x, z, y, 1 - c))


def turned(array):
    return move(array, lambda x, z, y, c: (z, x, y, c))


def wave_table(length):
    period = 2 * length
    freq = 2 * np.arange(length) + 1
    steps = np.arange(length)
    angle = (steps[:, None] * freq[None, :] % (2 * period)) * (math.pi / period)
    table = np.concatenate([np.cos(angle), -np.sin(angle)], axis=1)
    high = table.astype(jnp.bfloat16)
    low = (table - high.astype(np.float64)).astype(jnp.bfloat16)
    return high, low


def call(kernel, out_shape, *args, scratch=(), in_hbm=(), time=2.0):
    specs, operands = [], []
    for place, arg in enumerate(args):
        if place in in_hbm:
            specs.append(pl.BlockSpec(memory_space=pl.ANY))
            operands.append(pltpu.with_memory_space_constraint(arg, pltpu.HBM))
        else:
            specs.append(pl.BlockSpec(memory_space=pltpu.VMEM))
            operands.append(pltpu.with_memory_space_constraint(arg, pltpu.VMEM))
    return pl.pallas_call(
        kernel,
        out_shape=out_shape,
        in_specs=specs,
        out_specs=jax.tree.map(lambda _: pl.BlockSpec(memory_space=pltpu.VMEM), out_shape),
        scratch_shapes=list(scratch),
        cost_estimate=pl.CostEstimate(
            flops=int(time * WEIGHT), transcendentals=0, bytes_accessed=int(time * 3.5e6)
        ),
        compiler_params=pltpu.CompilerParams(vmem_limit_bytes=VMEM_LIMIT),
    )(*operands)


def shape(dims, dtype):
    return jax.ShapeDtypeStruct(dims, dtype)


def kept(dims, dtype):
    return pltpu.VMEM(dims, dtype)


def pack_kernel(feat_ref, filt_ref, taps_ref, p0, p1, p2, p3, taps_out, held, taps_held):
    x = coords()[0]
    for stream in range(4):
        block = feat_ref[stream] if stream < 3 else filt_ref[...]
        flipped = block.T
        for quarter in range(4):
            held[quarter, stream] = flipped[quarter * 64 : quarter * 64 + 64]
    for by, out in enumerate((p0, p1, p2, p3)):
        out[...] = held[lax.rem(x + by, 4)]
    rows = jnp.zeros((128, 256), F32)
    taps_held[0] = rows
    for stream in range(3):
        taps_held[0, stream * 8 : stream * 8 + TAPS, :] = taps_ref[stream]
    columns = taps_held[0].T
    for quarter in range(4):
        taps_held[1 + quarter, 0:64, 0:128] = columns[quarter * 64 : quarter * 64 + 64]
    taps_out[...] = taps_held[1 + x, 0:64, 0:128]


def lift_kernel(g0, g1, g2, g3, weight, behind, whole_out, send_out, gathered, rows, sem):
    x, z, y, c = coords()
    copy = pltpu.make_async_copy(weight.at[:, :, 1 - c, x], rows, sem)
    copy.start()
    for by, block in enumerate((g0, g1, g2, g3)):
        gathered[lax.rem(x + 4 - by, 4)] = block[...]
    whole = gathered[...].reshape(512, 256)
    whole_out[...] = whole
    copy.wait()
    for zd in range(NZ):
        part = lax.dot_general(
            rows[zd].reshape(256, 256), whole, NT, preferred_element_type=F32
        )
        send_out[zd] = part.astype(BF16).reshape(NY, 64, 512)


def sum_core_kernel(recv, whole, weight, own_out, s1, s2, s3, rows, sem):
    x, z, y, c = coords()
    copy = pltpu.make_async_copy(weight.at[:, :, c, x], rows, sem)
    copy.start()
    copy.wait()
    for by, out in enumerate((own_out, s1, s2, s3)):
        zd = lax.rem(z + by, 4)
        part = lax.dot_general(
            rows[zd].reshape(256, 256), whole[...], NT, preferred_element_type=F32
        )
        total = part.reshape(NY, 64, 512) + recv[zd].astype(F32)
        out[...] = total.astype(out.dtype)


def sum_z_kernel(own, r1, r2, r3, own_out, s1, s2, s3):
    y = coords()[2]
    for by, out in enumerate((own_out, s1, s2, s3)):
        yd = lax.rem(y + by, 4)
        total = (
            own[yd] + r1[yd].astype(F32) + (r2[yd].astype(F32) + r3[yd].astype(F32))
        )
        out[...] = total.astype(out.dtype)


def later(values, by, lane):
    if by == 0:
        return values
    return jnp.where(lane >= by, pltpu.roll(values, by, 1), 0.0)


def sooner(values, by, lane):
    if by == 0:
        return values
    return jnp.where(lane < 512 - by, pltpu.roll(values, 512 - by, 1), 0.0)


def split(values):
    high = values.astype(BF16)
    return high, (values - high.astype(F32)).astype(BF16)


def forward(rows, high, low):
    return jnp.dot(rows, high[...], preferred_element_type=F32) + jnp.dot(
        rows, low[...], preferred_element_type=F32
    )


def backward(spectra, high, low):
    count = spectra.shape[0]
    big, small = split(spectra)
    first = lax.dot_general(
        jnp.concatenate([big, small], axis=0), high[...], NT, preferred_element_type=F32
    )
    second = lax.dot_general(big, low[...], NT, preferred_element_type=F32)
    return (first[:count] + first[count:] + second) * (1.0 / 512)


def pre_kernel(p0, r1, r2, r3, taps, high, low, behind, mixed_out, conv_out, long_out, spec_out, feat_out, held):
    x = coords()[0]
    for by, block in enumerate((p0, r1, r2, r3)):
        held[lax.rem(x + 4 - by, 4)] = block[...]
    lane = lax.broadcasted_iota(jnp.int32, (64, 512), 1)
    convs = []
    for stream in range(3):
        feats = jnp.concatenate([held[b, stream] for b in range(4)], axis=1)
        feat_out[stream] = feats
        wide = feats.astype(F32)
        total = taps[:, stream * 8 : stream * 8 + 1] * wide
        for tap in range(1, TAPS):
            column = stream * 8 + tap
            total = total + taps[:, column : column + 1] * later(wide, tap, lane)
        conv_out[stream] = total
        convs.append(total)
    gated = (convs[1] * convs[2]).astype(BF16)
    filt = jnp.concatenate([held[b, 3] for b in range(4)], axis=1)
    spec = forward(jnp.concatenate([gated, filt], axis=0), high, low)
    spec_out[...] = spec
    gr, gi = spec[:64, :512], spec[:64, 512:]
    hr, hi = spec[64:, :512], spec[64:, 512:]
    product = jnp.concatenate([gr * hr - gi * hi, gr * hi + gi * hr], axis=1)
    long = backward(product, high, low)
    long_out[...] = long
    mixed_out[...] = (convs[0] * long).astype(BF16)


def post_kernel(own, r1, r2, r3, conv, long, spec, feats, taps, high, low, o0, o1, o2, o3, held):
    x = coords()[0]
    lane = lax.broadcasted_iota(jnp.int32, (64, 512), 1)
    grad_mixed = own[...] + r1[...].astype(F32) + (r2[...].astype(F32) + r3[...].astype(F32))
    grad_long = (grad_mixed * conv[0]).astype(BF16)
    lspec = forward(grad_long, high, low)
    lr, li = lspec[:, :512], lspec[:, 512:]
    gr, gi = spec[:64, :512], spec[:64, 512:]
    hr, hi = spec[64:, :512], spec[64:, 512:]
    to_gated = jnp.concatenate([hr * lr + hi * li, hr * li - hi * lr], axis=1)
    to_filter = jnp.concatenate([gr * lr + gi * li, gr * li - gi * lr], axis=1)
    both = backward(jnp.concatenate([to_gated, to_filter], axis=0), high, low)
    grad_gated, grad_filter = both[:64], both[64:]
    grad_conv = (grad_mixed * long[...], grad_gated * conv[2], grad_gated * conv[1])
    slot = lax.broadcasted_iota(jnp.int32, (64, 128), 1)
    sums = jnp.zeros((64, 128), F32)
    for stream in range(3):
        wide = feats[stream].astype(F32)
        total = None
        for tap in range(TAPS):
            column = stream * 8 + tap
            term = taps[:, column : column + 1] * sooner(grad_conv[stream], tap, lane)
            total = term if total is None else total + term
            row = jnp.sum(grad_conv[stream] * later(wide, tap, lane), axis=1, keepdims=True)
            sums = jnp.where(slot == column, row, sums)
        rounded = total.astype(BF16)
        for b in range(4):
            held[b, stream] = rounded[:, b * 128 : b * 128 + 128]
    high_part, low_part = split(grad_filter)
    sums_high, sums_low = split(sums)
    sums_both = sums_high.astype(F32) + pltpu.roll(sums_low.astype(F32), 32, 1)
    for b in range(4):
        held[b, 3] = high_part[:, b * 128 : b * 128 + 128]
        held[b, 4] = low_part[:, b * 128 : b * 128 + 128]
        held[b, 5] = sums_both.astype(BF16)
    for by, out in enumerate((o0, o1, o2, o3)):
        out[...] = held[lax.rem(x + by, 4)]


def out_kernel(o0, r1, r2, r3, feat_out, taps_out, filt_out, held):
    x = coords()[0]
    for by, block in enumerate((o0, r1, r2, r3)):
        held[lax.rem(x + 4 - by, 4)] = block[...]
    for stream in range(3):
        columns = jnp.concatenate([held[q, stream] for q in range(4)], axis=0)
        feat_out[stream] = columns.T
    filt = jnp.concatenate(
        [held[q, 3].astype(F32) + held[q, 4].astype(F32) for q in range(4)], axis=0
    )
    filt_out[...] = filt.T
    sums = jnp.concatenate([held[q, 5].astype(F32) for q in range(4)], axis=0)
    sums = sums + pltpu.roll(sums, 96, 1)
    rows = sums.T
    for stream in range(3):
        taps_out[stream] = rows[stream * 8 : stream * 8 + TAPS]


def weight_kernel(mine, theirs, whole, out):
    x, z, y, c = coords()
    for half, blocks in enumerate((mine, theirs)):
        core = c if half == 0 else 1 - c
        for across in range(4):
            src = lax.rem(z + 4 - across, 4)
            part = jnp.dot(
                blocks[across].reshape(256, 512), whole[...], preferred_element_type=F32
            )
            for along in range(4):
                yd = lax.rem(y + 4 - along, 4)
                start = pl.multiple_of(yd * 512 + core * 256 + src * 64, 64)
                out[pl.ds(start, 64), :] = part[along * 64 : along * 64 + 64]


def local(high, low, features, short_kernel, long_filter, out_weight, grad_out):
    high, low = jnp.asarray(high), jnp.asarray(low)
    weight = out_weight.reshape(NZ, NY, NC, NX, 64, 256)
    g = [grad_out] + [along_x(grad_out, k) for k in (1, 2, 3)]
    *pay, taps = call(
        pack_kernel,
        [kept((4, 64, 128), BF16)] * 4 + [kept((64, 128), F32)],
        features,
        long_filter,
        short_kernel,
        scratch=[pltpu.VMEM((4, 4, 64, 128), BF16), pltpu.VMEM((5, 128, 256), F32)],
    )
    got = [pay[0]] + [along_x(pay[k], k) for k in (1, 2, 3)]
    whole, send = call(
        lift_kernel,
        [kept((512, 256), BF16), kept((NZ, NY, 64, 512), BF16)],
        *g,
        weight,
        taps,
        in_hbm=(4,),
        scratch=[
            pltpu.VMEM((4, 128, 256), BF16),
            pltpu.VMEM((NZ, NY, 64, 256), BF16),
            pltpu.SemaphoreType.DMA,
        ],
    )
    recv = other_core(send)
    own, *sends = call(
        sum_core_kernel,
        [kept((NY, 64, 512), F32)] + [kept((NY, 64, 512), BF16)] * 3,
        recv,
        whole,
        weight,
        in_hbm=(2,),
        scratch=[pltpu.VMEM((NZ, NY, 64, 256), BF16), pltpu.SemaphoreType.DMA],
    )
    recvs = [along_z(sends[k - 1], k) for k in (1, 2, 3)]
    mixed, conv, long, spec, feats = call(
        pre_kernel,
        [
            kept((64, 512), BF16),
            kept((3, 64, 512), F32),
            kept((64, 512), F32),
            kept((128, 1024), F32),
            kept((3, 64, 512), BF16),
        ],
        *got,
        taps,
        high,
        low,
        sends[2],
        scratch=[pltpu.VMEM((4, 4, 64, 128), BF16)],
        time=3.0,
    )
    moved = turned(mixed)
    column = jnp.stack([moved] + [along_y(moved, k) for k in (1, 2, 3)])
    mine = jnp.stack([column] + [along_z(column, k) for k in (1, 2, 3)])
    theirs = other_core(mine)
    own, *sends = call(
        sum_z_kernel,
        [kept((64, 512), F32)] + [kept((64, 512), BF16)] * 3,
        own,
        *recvs,
    )
    recvs = [along_y(sends[k - 1], k) for k in (1, 2, 3)]
    outs = call(
        post_kernel,
        [kept((6, 64, 128), BF16)] * 4,
        own,
        *recvs,
        conv,
        long,
        spec,
        feats,
        taps,
        high,
        low,
        scratch=[pltpu.VMEM((4, 6, 64, 128), BF16)],
        time=5.0,
    )
    backs = [outs[0]] + [along_x(outs[k], k) for k in (1, 2, 3)]
    grad_features, grad_kernel, grad_filter = call(
        out_kernel,
        [shape((3, 128, 256), BF16), shape((3, TAPS, 256), F32), shape((128, 256), F32)],
        *backs,
        scratch=[pltpu.VMEM((4, 6, 64, 128), BF16)],
    )
    grad_weight = call(weight_kernel, shape((2048, 256), F32), mine, theirs, whole, time=3.0)
    return grad_features, grad_kernel, grad_filter, grad_weight


def solution(mesh):
    high, low = wave_table(512)
    return jax.shard_map(
        functools.partial(local, high, low),
        mesh=mesh,
        in_specs=(
            P(None, "ctx", "ch"),
            P(None, None, "ch"),
            P("ctx", "ch"),
            P(None, "ch"),
            P("ctx", "ch"),
        ),
        out_specs=(P(None, "ctx", "ch"), P(None, None, "ch"), P("ctx", "ch"), P("ctx", "ch")),
        check_vma=False,
    )
```

```python
import functools
import math

import jax
import jax.numpy as jnp
import numpy as np
from jax import lax
from jax.experimental import pallas as pl
from jax.experimental.pallas import tpu as pltpu
from jax.sharding import PartitionSpec as P

F32 = jnp.float32
BF16 = jnp.bfloat16
NX, NZ, NY, NC = 4, 4, 4, 2
TAPS = 7
NT = (((1,), (1,)), ((), ()))
VMEM_LIMIT = 20 * 1024 * 1024
WEIGHT = 3.5e10


def coords():
    x = lax.axis_index("ctx")
    ch = lax.axis_index("ch")
    return x, ch // 8, lax.rem(ch // 2, 4), lax.rem(ch, 2)


def flat(x, z, y, c):
    return ((x * NZ + z) * NY + y) * NC + c


def move(array, rule):
    pairs = []
    for x in range(NX):
        for z in range(NZ):
            for y in range(NY):
                for c in range(NC):
                    pairs.append((flat(x, z, y, c), flat(*rule(x, z, y, c))))
    return lax.ppermute(array, ("ctx", "ch"), pairs)


def along_x(array, by):
    return move(array, lambda x, z, y, c: ((x + by) % NX, z, y, c))


def along_z(array, by):
    return move(array, lambda x, z, y, c: (x, (z + by) % NZ, y, c))


def along_y(array, by):
    return move(array, lambda x, z, y, c: (x, z, (y + by) % NY, c))


def other_core(array):
    return move(array, lambda x, z, y, c: (x, z, y, 1 - c))


def turned(array):
    return move(array, lambda x, z, y, c: (z, x, y, c))


def wave_table(length):
    period = 2 * length
    freq = 2 * np.arange(length) + 1
    steps = np.arange(length)
    angle = (steps[:, None] * freq[None, :] % (2 * period)) * (math.pi / period)
    table = np.concatenate([np.cos(angle), -np.sin(angle)], axis=1)
    high = table.astype(jnp.bfloat16)
    low = (table - high.astype(np.float64)).astype(jnp.bfloat16)
    return high, low


def call(kernel, out_shape, *args, scratch=(), in_hbm=(), time=2.0):
    specs, operands = [], []
    for place, arg in enumerate(args):
        if place in in_hbm:
            specs.append(pl.BlockSpec(memory_space=pl.ANY))
            operands.append(pltpu.with_memory_space_constraint(arg, pltpu.HBM))
        else:
            specs.append(pl.BlockSpec(memory_space=pltpu.VMEM))
            operands.append(pltpu.with_memory_space_constraint(arg, pltpu.VMEM))
    return pl.pallas_call(
        kernel,
        out_shape=out_shape,
        name=kernel.__name__,
        in_specs=specs,
        out_specs=jax.tree.map(lambda _: pl.BlockSpec(memory_space=pltpu.VMEM), out_shape),
        scratch_shapes=list(scratch),
        cost_estimate=pl.CostEstimate(
            flops=int(time * WEIGHT), transcendentals=0, bytes_accessed=int(time * 3.5e6)
        ),
        compiler_params=pltpu.CompilerParams(vmem_limit_bytes=VMEM_LIMIT),
    )(*operands)


def shape(dims, dtype):
    return jax.ShapeDtypeStruct(dims, dtype)


def kept(dims, dtype):
    return pltpu.VMEM(dims, dtype)


def pack_kernel(
    feat_hbm,
    filt_hbm,
    taps_hbm,
    grad_hbm,
    p0,
    p1,
    p2,
    p3,
    taps_out,
    feat_ref,
    filt_ref,
    taps_ref,
    grad_ref,
    held,
    taps_held,
    sems,
):
    x = coords()[0]
    copies = []
    for place, (src, dst) in enumerate(
        (
            (feat_hbm, feat_ref),
            (filt_hbm, filt_ref),
            (grad_hbm, grad_ref),
            (taps_hbm, taps_ref),
        )
    ):
        copy = pltpu.make_async_copy(src, dst, sems.at[place])
        copy.start()
        copies.append(copy)
    for copy in copies:
        copy.wait()
    for stream in range(4):
        block = feat_ref[stream] if stream < 3 else filt_ref[...]
        flipped = block.T
        for quarter in range(4):
            held[quarter, stream] = flipped[quarter * 64 : quarter * 64 + 64]
    for by, out in enumerate((p0, p1, p2, p3)):
        out[0:4] = held[lax.rem(x + by, 4)]
        for row in range(2):
            for column in range(2):
                out[4 + 2 * row + column] = grad_ref[
                    row * 64 : row * 64 + 64, column * 128 : column * 128 + 128
                ]
    taps_held[0] = jnp.zeros((128, 256), F32)
    for stream in range(3):
        taps_held[0, stream * 8 : stream * 8 + TAPS, :] = taps_ref[stream]
    columns = taps_held[0].T
    for quarter in range(4):
        taps_held[1 + quarter, 0:64, 0:128] = columns[quarter * 64 : quarter * 64 + 64]
    taps_out[...] = taps_held[1 + x, 0:64, 0:128]


def fetch_kernel(weight, behind, out, sems):
    x, z, y, c = coords()
    copies = []
    for half in range(2):
        core = c if half == 0 else 1 - c
        copy = pltpu.make_async_copy(weight.at[:, :, core, x], out.at[half], sems.at[half])
        copy.start()
        copies.append(copy)
    for copy in copies:
        copy.wait()


def lift_kernel(p0, r1, r2, r3, rows, whole_out, send_out, gathered):
    x, z, y, c = coords()
    for by, block in enumerate((p0, r1, r2, r3)):
        slot = lax.rem(x + 4 - by, 4)
        for row in range(2):
            for column in range(2):
                gathered[
                    slot, row * 64 : row * 64 + 64, column * 128 : column * 128 + 128
                ] = block[4 + 2 * row + column]
    whole = gathered[...].reshape(512, 256)
    whole_out[...] = whole
    for zd in range(NZ):
        part = lax.dot_general(
            rows[1, zd].reshape(256, 256), whole, NT, preferred_element_type=F32
        )
        send_out[zd] = part.astype(BF16).reshape(NY, 64, 512)


def sum_core_kernel(recv, whole, rows, behind, own_out, s1, s2, s3):
    x, z, y, c = coords()
    for by, out in enumerate((own_out, s1, s2, s3)):
        zd = lax.rem(z + by, 4)
        part = lax.dot_general(
            rows[0, zd].reshape(256, 256), whole[...], NT, preferred_element_type=F32
        )
        total = part.reshape(NY, 64, 512) + recv[zd].astype(F32)
        out[...] = total.astype(out.dtype)


def sum_z_kernel(own, r1, r2, r3, behind, own_out, s1, s2, s3):
    y = coords()[2]
    for by, out in enumerate((own_out, s1, s2, s3)):
        yd = lax.rem(y + by, 4)
        total = (
            own[yd] + r1[yd].astype(F32) + (r2[yd].astype(F32) + r3[yd].astype(F32))
        )
        out[...] = total.astype(out.dtype)


def later(values, by, lane):
    if by == 0:
        return values
    return jnp.where(lane >= by, pltpu.roll(values, by, 1), 0.0)


def sooner(values, by, lane):
    if by == 0:
        return values
    return jnp.where(lane < 512 - by, pltpu.roll(values, 512 - by, 1), 0.0)


def split(values):
    high = values.astype(BF16)
    return high, (values - high.astype(F32)).astype(BF16)


def forward(rows, high, low):
    return jnp.dot(rows, high[...], preferred_element_type=F32) + jnp.dot(
        rows, low[...], preferred_element_type=F32
    )


def backward(spectra, high, low):
    count = spectra.shape[0]
    big, small = split(spectra)
    first = lax.dot_general(
        jnp.concatenate([big, small], axis=0), high[...], NT, preferred_element_type=F32
    )
    second = lax.dot_general(big, low[...], NT, preferred_element_type=F32)
    return (first[:count] + first[count:] + second) * (1.0 / 512)


def pre_kernel(p0, r1, r2, r3, taps, high, low, behind, mixed_out, conv_out, long_out, spec_out, feat_out, held):
    x = coords()[0]
    for by, block in enumerate((p0, r1, r2, r3)):
        held[lax.rem(x + 4 - by, 4)] = block[0:4]
    lane = lax.broadcasted_iota(jnp.int32, (64, 512), 1)
    convs = []
    for stream in range(3):
        feats = jnp.concatenate([held[b, stream] for b in range(4)], axis=1)
        feat_out[stream] = feats
        wide = feats.astype(F32)
        total = taps[:, stream * 8 : stream * 8 + 1] * wide
        for tap in range(1, TAPS):
            column = stream * 8 + tap
            total = total + taps[:, column : column + 1] * later(wide, tap, lane)
        conv_out[stream] = total
        convs.append(total)
    gated = (convs[1] * convs[2]).astype(BF16)
    filt = jnp.concatenate([held[b, 3] for b in range(4)], axis=1)
    spec = forward(jnp.concatenate([gated, filt], axis=0), high, low)
    spec_out[...] = spec
    gr, gi = spec[:64, :512], spec[:64, 512:]
    hr, hi = spec[64:, :512], spec[64:, 512:]
    product = jnp.concatenate([gr * hr - gi * hi, gr * hi + gi * hr], axis=1)
    long = backward(product, high, low)
    long_out[...] = long
    mixed_out[...] = (convs[0] * long).astype(BF16)


def post_kernel(own, r1, r2, r3, conv, long, spec, feats, taps, high, low, o0, o1, o2, o3, held):
    x = coords()[0]
    lane = lax.broadcasted_iota(jnp.int32, (64, 512), 1)
    grad_mixed = own[...] + r1[...].astype(F32) + (r2[...].astype(F32) + r3[...].astype(F32))
    grad_long = (grad_mixed * conv[0]).astype(BF16)
    lspec = forward(grad_long, high, low)
    lr, li = lspec[:, :512], lspec[:, 512:]
    gr, gi = spec[:64, :512], spec[:64, 512:]
    hr, hi = spec[64:, :512], spec[64:, 512:]
    to_gated = jnp.concatenate([hr * lr + hi * li, hr * li - hi * lr], axis=1)
    to_filter = jnp.concatenate([gr * lr + gi * li, gr * li - gi * lr], axis=1)
    both = backward(jnp.concatenate([to_gated, to_filter], axis=0), high, low)
    grad_gated, grad_filter = both[:64], both[64:]
    grad_conv = (grad_mixed * long[...], grad_gated * conv[2], grad_gated * conv[1])
    slot = lax.broadcasted_iota(jnp.int32, (64, 128), 1)
    sums = jnp.zeros((64, 128), F32)
    for stream in range(3):
        wide = feats[stream].astype(F32)
        total = None
        for tap in range(TAPS):
            column = stream * 8 + tap
            ahead = sooner(grad_conv[stream], tap, lane)
            term = taps[:, column : column + 1] * ahead
            total = term if total is None else total + term
            row = jnp.sum(ahead * wide, axis=1, keepdims=True)
            sums = jnp.where(slot == column, row, sums)
        rounded = total.astype(BF16)
        for b in range(4):
            held[b, stream] = rounded[:, b * 128 : b * 128 + 128]
    high_part, low_part = split(grad_filter)
    sums_high, sums_low = split(sums)
    sums_both = sums_high.astype(F32) + pltpu.roll(sums_low.astype(F32), 32, 1)
    for b in range(4):
        held[b, 3] = high_part[:, b * 128 : b * 128 + 128]
        held[b, 4] = low_part[:, b * 128 : b * 128 + 128]
        held[b, 5] = sums_both.astype(BF16)
    for by, out in enumerate((o0, o1, o2, o3)):
        out[...] = held[lax.rem(x + by, 4)]


def out_kernel(o0, r1, r2, r3, feat_out, taps_out, filt_out, held):
    x = coords()[0]
    for by, block in enumerate((o0, r1, r2, r3)):
        held[lax.rem(x + 4 - by, 4)] = block[...]
    for stream in range(3):
        columns = jnp.concatenate([held[q, stream] for q in range(4)], axis=0)
        feat_out[stream] = columns.T
    filt = jnp.concatenate(
        [held[q, 3].astype(F32) + held[q, 4].astype(F32) for q in range(4)], axis=0
    )
    filt_out[...] = filt.T
    sums = jnp.concatenate([held[q, 5].astype(F32) for q in range(4)], axis=0)
    sums = sums + pltpu.roll(sums, 96, 1)
    rows = sums.T
    for stream in range(3):
        taps_out[stream] = rows[stream * 8 : stream * 8 + TAPS]


def relay_kernel(block, behind, out):
    out[...] = block[...]


def collect_kernel(b0, b1, b2, b3, out):
    for place, block in enumerate((b0, b1, b2, b3)):
        out[place] = block[...]


def weight_kernel(mine, theirs, whole, out):
    x, z, y, c = coords()
    for half, blocks in enumerate((mine, theirs)):
        core = c if half == 0 else 1 - c
        for along in range(4):
            yd = lax.rem(y + 4 - along, 4)
            part = jnp.dot(
                blocks[along].reshape(256, 512), whole[...], preferred_element_type=F32
            )
            for across in range(4):
                src = lax.rem(z + 4 - across, 4)
                start = pl.multiple_of(yd * 512 + core * 256 + src * 64, 64)
                out[pl.ds(start, 64), :] = part[across * 64 : across * 64 + 64]


def local(high, low, features, short_kernel, long_filter, out_weight, grad_out):
    high, low = jnp.asarray(high), jnp.asarray(low)
    weight = out_weight.reshape(NZ, NY, NC, NX, 64, 256)
    *pay, taps = call(
        pack_kernel,
        [kept((8, 64, 128), BF16)] * 4 + [kept((64, 128), F32)],
        features,
        long_filter,
        short_kernel,
        grad_out,
        in_hbm=(0, 1, 2, 3),
        scratch=[
            pltpu.VMEM((3, 128, 256), BF16),
            pltpu.VMEM((128, 256), BF16),
            pltpu.VMEM((3, TAPS, 256), F32),
            pltpu.VMEM((128, 256), BF16),
            pltpu.VMEM((4, 4, 64, 128), BF16),
            pltpu.VMEM((5, 128, 256), F32),
            pltpu.SemaphoreType.DMA((4,)),
        ],
    )
    got = [pay[0]] + [along_x(pay[k], k) for k in (1, 2, 3)]
    rows = call(
        fetch_kernel,
        kept((2, NZ, NY, 64, 256), BF16),
        weight,
        taps,
        in_hbm=(0,),
        scratch=[pltpu.SemaphoreType.DMA((2,))],
    )
    whole, send = call(
        lift_kernel,
        [kept((512, 256), BF16), kept((NZ, NY, 64, 512), BF16)],
        *got,
        rows,
        scratch=[pltpu.VMEM((4, 128, 256), BF16)],
    )
    recv = other_core(send)
    mixed, conv, long, spec, feats = call(
        pre_kernel,
        [
            kept((64, 512), BF16),
            kept((3, 64, 512), F32),
            kept((64, 512), F32),
            kept((128, 1024), F32),
            kept((3, 64, 512), BF16),
        ],
        *got,
        taps,
        high,
        low,
        whole,
        scratch=[pltpu.VMEM((4, 4, 64, 128), BF16)],
    )
    own, *sends = call(
        sum_core_kernel,
        [kept((NY, 64, 512), F32)] + [kept((NY, 64, 512), BF16)] * 3,
        recv,
        whole,
        rows,
        mixed,
    )
    recvs = [along_z(sends[k - 1], k) for k in (1, 2, 3)]
    moved = call(relay_kernel, kept((64, 512), BF16), turned(mixed), sends[2], time=0.0)
    column = call(
        collect_kernel,
        kept((4, 64, 512), BF16),
        moved,
        *[along_z(moved, k) for k in (1, 2, 3)],
        time=0.0,
    )
    mine = call(
        collect_kernel,
        kept((4, 4, 64, 512), BF16),
        column,
        *[along_y(column, k) for k in (1, 2, 3)],
        time=0.0,
    )
    theirs = other_core(mine)
    own, *sends = call(
        sum_z_kernel,
        [kept((64, 512), F32)] + [kept((64, 512), BF16)] * 3,
        own,
        *recvs,
        column,
        time=0.3,
    )
    recvs = [along_y(sends[k - 1], k) for k in (1, 2, 3)]
    outs = call(
        post_kernel,
        [kept((6, 64, 128), BF16)] * 4,
        own,
        *recvs,
        conv,
        long,
        spec,
        feats,
        taps,
        high,
        low,
        scratch=[pltpu.VMEM((4, 6, 64, 128), BF16)],
        time=3.0,
    )
    backs = [outs[0]] + [along_x(outs[k], k) for k in (1, 2, 3)]
    grad_features, grad_kernel, grad_filter = call(
        out_kernel,
        [shape((3, 128, 256), BF16), shape((3, TAPS, 256), F32), shape((128, 256), F32)],
        *backs,
        scratch=[pltpu.VMEM((4, 6, 64, 128), BF16)],
        time=1.0,
    )
    grad_weight = call(weight_kernel, shape((2048, 256), F32), mine, theirs, whole)
    return grad_features, grad_kernel, grad_filter, grad_weight


def solution(mesh):
    high, low = wave_table(512)
    return jax.shard_map(
        functools.partial(local, high, low),
        mesh=mesh,
        in_specs=(
            P(None, "ctx", "ch"),
            P(None, None, "ch"),
            P("ctx", "ch"),
            P(None, "ch"),
            P("ctx", "ch"),
        ),
        out_specs=(P(None, "ctx", "ch"), P(None, None, "ch"), P("ctx", "ch"), P("ctx", "ch")),
        check_vma=False,
    )
```

```python
import functools
import math

import jax
import jax.numpy as jnp
import numpy as np
from jax import lax
from jax.experimental import pallas as pl
from jax.experimental.pallas import tpu as pltpu
from jax.sharding import PartitionSpec as P

F32 = jnp.float32
BF16 = jnp.bfloat16
NX, NZ, NY, NC = 4, 4, 4, 2
TAPS = 7
NT = (((1,), (1,)), ((), ()))
VMEM_LIMIT = 20 * 1024 * 1024
WEIGHT = 3.5e10
TIMES = dict(
    pack=2, fetch=2, lift=2, core=2, pre=2, relay=0.3, collect=0.3, sum=0.3, post=3, out=1, weight=2, near=0
)


def coords():
    x = lax.axis_index("ctx")
    ch = lax.axis_index("ch")
    return x, ch // 8, lax.rem(ch // 2, 4), lax.rem(ch, 2)


def flat(x, z, y, c):
    return ((x * NZ + z) * NY + y) * NC + c


def move(array, rule):
    pairs = []
    for x in range(NX):
        for z in range(NZ):
            for y in range(NY):
                for c in range(NC):
                    pairs.append((flat(x, z, y, c), flat(*rule(x, z, y, c))))
    return lax.ppermute(array, ("ctx", "ch"), pairs)


def along_x(array, by):
    return move(array, lambda x, z, y, c: ((x + by) % NX, z, y, c))


def along_z(array, by):
    return move(array, lambda x, z, y, c: (x, (z + by) % NZ, y, c))


def along_y(array, by):
    return move(array, lambda x, z, y, c: (x, z, (y + by) % NY, c))


def other_core(array):
    return move(array, lambda x, z, y, c: (x, z, y, 1 - c))


def wave_table(length):
    period = 2 * length
    freq = 2 * np.arange(length) + 1
    steps = np.arange(length)
    angle = (steps[:, None] * freq[None, :] % (2 * period)) * (math.pi / period)
    table = np.concatenate([np.cos(angle), -np.sin(angle)], axis=1)
    high = table.astype(jnp.bfloat16)
    low = (table - high.astype(np.float64)).astype(jnp.bfloat16)
    return high, low


def call(
    kernel, out_shape, *args, scratch=(), in_hbm=(), out_hbm=False, aliases=None, time=2.0
):
    out_space = pl.ANY if out_hbm else pltpu.VMEM
    specs, operands = [], []
    for place, arg in enumerate(args):
        if place in in_hbm:
            specs.append(pl.BlockSpec(memory_space=pl.ANY))
            operands.append(pltpu.with_memory_space_constraint(arg, pltpu.HBM))
        else:
            specs.append(pl.BlockSpec(memory_space=pltpu.VMEM))
            operands.append(pltpu.with_memory_space_constraint(arg, pltpu.VMEM))
    return pl.pallas_call(
        kernel,
        out_shape=out_shape,
        name=kernel.__name__,
        in_specs=specs,
        out_specs=jax.tree.map(lambda _: pl.BlockSpec(memory_space=out_space), out_shape),
        scratch_shapes=list(scratch),
        input_output_aliases=aliases or {},
        cost_estimate=pl.CostEstimate(
            flops=int(time * WEIGHT), transcendentals=0, bytes_accessed=int(time * 3.5e6)
        ),
        compiler_params=pltpu.CompilerParams(vmem_limit_bytes=VMEM_LIMIT),
    )(*operands)


def shape(dims, dtype):
    return jax.ShapeDtypeStruct(dims, dtype)


def kept(dims, dtype):
    return pltpu.VMEM(dims, dtype)


def pack_kernel(
    feat_hbm,
    filt_hbm,
    taps_hbm,
    grad_hbm,
    p0,
    p1,
    p2,
    p3,
    taps_out,
    feat_ref,
    filt_ref,
    taps_ref,
    grad_ref,
    held,
    square,
    sems,
):
    x = coords()[0]
    copies = []
    for place, (src, dst) in enumerate(
        (
            (feat_hbm, feat_ref),
            (filt_hbm, filt_ref),
            (taps_hbm, taps_ref),
            (grad_hbm, grad_ref),
        )
    ):
        copy = pltpu.make_async_copy(src, dst, sems.at[place])
        copy.start()
        copies.append(copy)
    square[0] = jnp.zeros((128, 256), F32)
    for copy in copies:
        copy.wait()
    for stream in range(4):
        flipped = (feat_ref[stream] if stream < 3 else filt_ref[...]).T
        for quarter in range(4):
            held[quarter, stream] = flipped[quarter * 64 : quarter * 64 + 64]
    for by, out in enumerate((p0, p1, p2, p3)):
        out[0:4] = held[lax.rem(x + by, 4)]
        for row in range(2):
            for column in range(2):
                out[4 + 2 * row + column] = grad_ref[
                    row * 64 : row * 64 + 64, column * 128 : column * 128 + 128
                ]
    for stream in range(3):
        square[0, stream * 8 : stream * 8 + TAPS, :] = taps_ref[stream]
    columns = square[0].T
    for quarter in range(4):
        square[1 + quarter, 0:64, 0:128] = columns[quarter * 64 : quarter * 64 + 64]
    taps_out[...] = square[1 + x, 0:64, 0:128]


def fetch_kernel(weight, high_hbm, low_hbm, behind, out, high, low, sems, table_sems):
    x, z, y, c = coords()
    copies = []
    for half in range(2):
        core = c if half == 0 else 1 - c
        for yd in range(NY):
            copies.append(
                pltpu.make_async_copy(
                    weight.at[:, yd, core, x], out.at[half, yd], sems.at[half, yd]
                )
            )
    copies.append(pltpu.make_async_copy(high_hbm, high, table_sems.at[0]))
    copies.append(pltpu.make_async_copy(low_hbm, low, table_sems.at[1]))
    for copy in copies:
        copy.start()
    for copy in copies:
        copy.wait()


def lift_kernel(p0, r1, r2, r3, rows, whole_out, send_out, gathered):
    x = coords()[0]
    for by, block in enumerate((p0, r1, r2, r3)):
        slot = lax.rem(x + 4 - by, 4)
        for row in range(2):
            for column in range(2):
                gathered[
                    slot, row * 64 : row * 64 + 64, column * 128 : column * 128 + 128
                ] = block[4 + 2 * row + column]
    whole = gathered[...].reshape(512, 256)
    whole_out[...] = whole
    for yd in range(NY):
        part = lax.dot_general(
            rows[1, yd].reshape(256, 256), whole, NT, preferred_element_type=F32
        )
        send_out[yd] = part.astype(BF16).reshape(NZ, 64, 512)


def sum_core_kernel(recv, whole, rows, behind, own_out, s1, s2, s3):
    y = coords()[2]
    for by, out in enumerate((own_out, s1, s2, s3)):
        yd = lax.rem(y + by, 4)
        part = lax.dot_general(
            rows[0, yd].reshape(256, 256), whole[...], NT, preferred_element_type=F32
        )
        total = part.reshape(NZ, 64, 512) + recv[yd].astype(F32)
        out[...] = total.astype(out.dtype)


def sum_y_kernel(own, r1, r2, r3, own_out, s1, s2, s3):
    z = coords()[1]
    for by, out in enumerate((own_out, s1, s2, s3)):
        zd = lax.rem(z + by, 4)
        total = (
            own[zd] + r1[zd].astype(F32) + (r2[zd].astype(F32) + r3[zd].astype(F32))
        )
        out[...] = total.astype(out.dtype)


def later(values, by, lane):
    if by == 0:
        return values
    return jnp.where(lane >= by, pltpu.roll(values, by, 1), 0.0)


def sooner(values, by, lane):
    if by == 0:
        return values
    return jnp.where(lane < 512 - by, pltpu.roll(values, 512 - by, 1), 0.0)


def split(values):
    high = values.astype(BF16)
    return high, (values - high.astype(F32)).astype(BF16)


def forward(rows, high, low):
    return jnp.dot(rows, high[...], preferred_element_type=F32) + jnp.dot(
        rows, low[...], preferred_element_type=F32
    )


def backward(spectra, high, low):
    count = spectra.shape[0]
    big, small = split(spectra)
    first = lax.dot_general(
        jnp.concatenate([big, small], axis=0), high[...], NT, preferred_element_type=F32
    )
    second = lax.dot_general(big, low[...], NT, preferred_element_type=F32)
    return (first[:count] + first[count:] + second) * (1.0 / 512)


def pre_kernel(p0, r1, r2, r3, taps, high, low, behind, mixed_out, conv_out, long_out, spec_out, feat_out, held):
    x = coords()[0]
    for by, block in enumerate((p0, r1, r2, r3)):
        held[lax.rem(x + 4 - by, 4)] = block[0:4]
    lane = lax.broadcasted_iota(jnp.int32, (64, 512), 1)
    convs = []
    for stream in range(3):
        feats = jnp.concatenate([held[b, stream] for b in range(4)], axis=1)
        feat_out[stream] = feats
        wide = feats.astype(F32)
        total = taps[:, stream * 8 : stream * 8 + 1] * wide
        for tap in range(1, TAPS):
            column = stream * 8 + tap
            total = total + taps[:, column : column + 1] * later(wide, tap, lane)
        conv_out[stream] = total
        convs.append(total)
    gated = (convs[1] * convs[2]).astype(BF16)
    filt = jnp.concatenate([held[b, 3] for b in range(4)], axis=1)
    spec = forward(jnp.concatenate([gated, filt], axis=0), high, low)
    spec_out[...] = spec
    gr, gi = spec[:64, :512], spec[:64, 512:]
    hr, hi = spec[64:, :512], spec[64:, 512:]
    product = jnp.concatenate([gr * hr - gi * hi, gr * hi + gi * hr], axis=1)
    long = backward(product, high, low)
    long_out[...] = long
    mixed_out[...] = (convs[0] * long).astype(BF16)


def post_kernel(own, r1, r2, r3, conv, long, spec, feats, taps, high, low, o0, o1, o2, o3, held):
    x = coords()[0]
    lane = lax.broadcasted_iota(jnp.int32, (64, 512), 1)
    grad_mixed = own[...] + r1[...].astype(F32) + (r2[...].astype(F32) + r3[...].astype(F32))
    grad_long = (grad_mixed * conv[0]).astype(BF16)
    lspec = forward(grad_long, high, low)
    lr, li = lspec[:, :512], lspec[:, 512:]
    gr, gi = spec[:64, :512], spec[:64, 512:]
    hr, hi = spec[64:, :512], spec[64:, 512:]
    to_gated = jnp.concatenate([hr * lr + hi * li, hr * li - hi * lr], axis=1)
    to_filter = jnp.concatenate([gr * lr + gi * li, gr * li - gi * lr], axis=1)
    both = backward(jnp.concatenate([to_gated, to_filter], axis=0), high, low)
    grad_gated, grad_filter = both[:64], both[64:]
    grad_conv = (grad_mixed * long[...], grad_gated * conv[2], grad_gated * conv[1])
    slot = lax.broadcasted_iota(jnp.int32, (64, 128), 1)
    sums = jnp.zeros((64, 128), F32)
    for stream in range(3):
        wide = feats[stream].astype(F32)
        total = None
        for tap in range(TAPS):
            column = stream * 8 + tap
            ahead = sooner(grad_conv[stream], tap, lane)
            term = taps[:, column : column + 1] * ahead
            total = term if total is None else total + term
            row = jnp.sum(ahead * wide, axis=1, keepdims=True)
            sums = jnp.where(slot == column, row, sums)
        rounded = total.astype(BF16)
        for b in range(4):
            held[b, stream] = rounded[:, b * 128 : b * 128 + 128]
    high_part, low_part = split(grad_filter)
    sums_high, sums_low = split(sums)
    sums_both = sums_high.astype(F32) + pltpu.roll(sums_low.astype(F32), 32, 1)
    for b in range(4):
        held[b, 3] = high_part[:, b * 128 : b * 128 + 128]
        held[b, 4] = low_part[:, b * 128 : b * 128 + 128]
        held[b, 5] = sums_both.astype(BF16)
    for by, out in enumerate((o0, o1, o2, o3)):
        out[...] = held[lax.rem(x + by, 4)]


def out_kernel(o0, r1, r2, r3, feat_out, taps_out, filt_out, held):
    x = coords()[0]
    for by, block in enumerate((o0, r1, r2, r3)):
        held[lax.rem(x + 4 - by, 4)] = block[...]
    for stream in range(3):
        columns = jnp.concatenate([held[q, stream] for q in range(4)], axis=0)
        feat_out[stream] = columns.T
    filt = jnp.concatenate(
        [held[q, 3].astype(F32) + held[q, 4].astype(F32) for q in range(4)], axis=0
    )
    filt_out[...] = filt.T
    sums = jnp.concatenate([held[q, 5].astype(F32) for q in range(4)], axis=0)
    sums = sums + pltpu.roll(sums, 96, 1)
    rows = sums.T
    for stream in range(3):
        taps_out[stream] = rows[stream * 8 : stream * 8 + TAPS]


def pair_kernel(b0, b1, out):
    out[0] = b0[...]
    out[1] = b1[...]


def route_kernel(near, far, o0, o1, o2, o3, held):
    x, z = coords()[:2]
    for back in range(4):
        held[lax.rem(z + 4 - back, 4)] = (near if back < 2 else far)[back % 2]
    for by, out in enumerate((o0, o1, o2, o3)):
        out[...] = held[lax.rem(x + by, 4)]


def collect_kernel(b0, b1, b2, b3, out):
    for place, block in enumerate((b0, b1, b2, b3)):
        out[place] = block[...]


def weight_half(blocks, whole, out, parts, sems, core):
    x, z, y, c = coords()
    stores = []
    for along in range(4):
        yd = lax.rem(y + 4 - along, 4)
        part = jnp.dot(
            blocks[along].reshape(256, 512), whole[...], preferred_element_type=F32
        )
        for across in range(4):
            src = lax.rem(x + 4 - across, 4)
            parts[along, src] = part[across * 64 : across * 64 + 64]
        store = pltpu.make_async_copy(parts.at[along], out.at[yd, core], sems.at[along])
        store.start()
        stores.append(store)
    for store in stores:
        store.wait()


def near_kernel(blocks, whole, out, parts, sems):
    weight_half(blocks, whole, out, parts, sems, coords()[3])


def far_kernel(blocks, whole, held, out, parts, sems):
    weight_half(blocks, whole, out, parts, sems, 1 - coords()[3])


def local(high, low, features, short_kernel, long_filter, out_weight, grad_out):
    high, low = jnp.asarray(high), jnp.asarray(low)
    weight = out_weight.reshape(NZ, NY, NC, NX, 64, 256)
    *pay, taps = call(
        pack_kernel,
        [kept((8, 64, 128), BF16)] * 4 + [kept((64, 128), F32)],
        features,
        long_filter,
        short_kernel,
        grad_out,
        in_hbm=(0, 1, 2, 3),
        scratch=[
            pltpu.VMEM((3, 128, 256), BF16),
            pltpu.VMEM((128, 256), BF16),
            pltpu.VMEM((3, TAPS, 256), F32),
            pltpu.VMEM((128, 256), BF16),
            pltpu.VMEM((4, 4, 64, 128), BF16),
            pltpu.VMEM((5, 128, 256), F32),
            pltpu.SemaphoreType.DMA((4,)),
        ],
        time=TIMES["pack"],
    )
    got = [pay[0]] + [along_x(pay[k], k) for k in (1, 2, 3)]
    rows, high, low = call(
        fetch_kernel,
        [kept((2, NY, NZ, 64, 256), BF16)] + [kept((512, 1024), BF16)] * 2,
        weight,
        high,
        low,
        taps,
        in_hbm=(0, 1, 2),
        scratch=[pltpu.SemaphoreType.DMA((2, NY)), pltpu.SemaphoreType.DMA((2,))],
        time=TIMES["fetch"],
    )
    whole, send = call(
        lift_kernel,
        [kept((512, 256), BF16), kept((NY, NZ, 64, 512), BF16)],
        *got,
        rows,
        scratch=[pltpu.VMEM((4, 128, 256), BF16)],
        time=TIMES["lift"],
    )
    recv = other_core(send)
    mixed, conv, long, spec, feats = call(
        pre_kernel,
        [
            kept((64, 512), BF16),
            kept((3, 64, 512), F32),
            kept((64, 512), F32),
            kept((128, 1024), F32),
            kept((3, 64, 512), BF16),
        ],
        *got,
        taps,
        high,
        low,
        whole,
        scratch=[pltpu.VMEM((4, 4, 64, 128), BF16)],
        time=TIMES["pre"],
    )
    own, *sends = call(
        sum_core_kernel,
        [kept((NZ, 64, 512), F32)] + [kept((NZ, 64, 512), BF16)] * 3,
        recv,
        whole,
        rows,
        mixed,
        time=TIMES["core"],
    )
    recvs = [along_y(sends[k - 1], k) for k in (1, 2, 3)]
    pair = call(
        pair_kernel, kept((2, 64, 512), BF16), mixed, along_z(mixed, 1), time=TIMES["relay"]
    )
    routed = call(
        route_kernel,
        [kept((64, 512), BF16)] * 4,
        pair,
        along_z(pair, 2),
        scratch=[pltpu.VMEM((4, 64, 512), BF16)],
        time=TIMES["relay"],
    )
    column = call(
        collect_kernel,
        kept((4, 64, 512), BF16),
        routed[0],
        *[along_x(routed[k], k) for k in (1, 2, 3)],
        time=TIMES["collect"],
    )
    mine = call(
        collect_kernel,
        kept((4, 4, 64, 512), BF16),
        column,
        *[along_y(column, k) for k in (1, 2, 3)],
        time=TIMES["collect"],
    )
    theirs = other_core(mine)
    own, *sends = call(
        sum_y_kernel,
        [kept((64, 512), F32)] + [kept((64, 512), BF16)] * 3,
        own,
        *recvs,
        time=TIMES["sum"],
    )
    recvs = [along_z(sends[k - 1], k) for k in (1, 2, 3)]
    outs = call(
        post_kernel,
        [kept((6, 64, 128), BF16)] * 4,
        own,
        *recvs,
        conv,
        long,
        spec,
        feats,
        taps,
        high,
        low,
        scratch=[pltpu.VMEM((4, 6, 64, 128), BF16)],
        time=TIMES["post"],
    )
    backs = [outs[0]] + [along_x(outs[k], k) for k in (1, 2, 3)]
    grad_features, grad_kernel, grad_filter = call(
        out_kernel,
        [shape((3, 128, 256), BF16), shape((3, TAPS, 256), F32), shape((128, 256), F32)],
        *backs,
        scratch=[pltpu.VMEM((4, 6, 64, 128), BF16)],
        time=TIMES["out"],
    )
    space = [pltpu.VMEM((NY, 4, 64, 256), F32), pltpu.SemaphoreType.DMA((NY,))]
    grad_weight = call(
        near_kernel,
        pltpu.HBM((NY, NC, 4, 64, 256), F32),
        mine,
        whole,
        out_hbm=True,
        scratch=space,
        time=TIMES["near"],
    )
    grad_weight = call(
        far_kernel,
        shape((NY, NC, 4, 64, 256), F32),
        theirs,
        whole,
        grad_weight,
        in_hbm=(2,),
        out_hbm=True,
        aliases={2: 0},
        scratch=space,
        time=TIMES["weight"],
    ).reshape(2048, 256)
    return grad_features, grad_kernel, grad_filter, grad_weight


def solution(mesh):
    high, low = wave_table(512)
    return jax.shard_map(
        functools.partial(local, high, low),
        mesh=mesh,
        in_specs=(
            P(None, "ctx", "ch"),
            P(None, None, "ch"),
            P("ctx", "ch"),
            P(None, "ch"),
            P("ctx", "ch"),
        ),
        out_specs=(P(None, "ctx", "ch"), P(None, None, "ch"), P("ctx", "ch"), P("ctx", "ch")),
        check_vma=False,
    )
```

```python
import functools
import math

import jax
import jax.numpy as jnp
import numpy as np
from jax import lax
from jax.experimental import pallas as pl
from jax.experimental.pallas import tpu as pltpu
from jax.sharding import PartitionSpec as P

F32 = jnp.float32
BF16 = jnp.bfloat16
NX, NZ, NY, NC = 4, 4, 4, 2
TAPS = 7
NT = (((1,), (1,)), ((), ()))
VMEM_LIMIT = 20 * 1024 * 1024
WEIGHT = 3.5e10
TIMES = dict(
    pack=2, fetch=2, lift=2, core=2, pre=2, relay=0, collect=0, sum=0.3, post=3, out=1, weight=2, near=0, pair=0, gate=0.3
)


def coords():
    x = lax.axis_index("ctx")
    ch = lax.axis_index("ch")
    return x, ch // 8, lax.rem(ch // 2, 4), lax.rem(ch, 2)


def flat(x, z, y, c):
    return ((x * NZ + z) * NY + y) * NC + c


def move(array, rule):
    pairs = []
    for x in range(NX):
        for z in range(NZ):
            for y in range(NY):
                for c in range(NC):
                    pairs.append((flat(x, z, y, c), flat(*rule(x, z, y, c))))
    return lax.ppermute(array, ("ctx", "ch"), pairs)


def along_x(array, by):
    return move(array, lambda x, z, y, c: ((x + by) % NX, z, y, c))


def along_z(array, by):
    return move(array, lambda x, z, y, c: (x, (z + by) % NZ, y, c))


def along_y(array, by):
    return move(array, lambda x, z, y, c: (x, z, (y + by) % NY, c))


def other_core(array):
    return move(array, lambda x, z, y, c: (x, z, y, 1 - c))


def wave_table(length):
    period = 2 * length
    freq = 2 * np.arange(length) + 1
    steps = np.arange(length)
    angle = (steps[:, None] * freq[None, :] % (2 * period)) * (math.pi / period)
    table = np.concatenate([np.cos(angle), -np.sin(angle)], axis=1)
    high = table.astype(jnp.bfloat16)
    low = (table - high.astype(np.float64)).astype(jnp.bfloat16)
    return high, low


def call(
    kernel, out_shape, *args, scratch=(), in_hbm=(), out_hbm=False, aliases=None, time=2.0
):
    out_space = pl.ANY if out_hbm else pltpu.VMEM
    specs, operands = [], []
    for place, arg in enumerate(args):
        if place in in_hbm:
            specs.append(pl.BlockSpec(memory_space=pl.ANY))
            operands.append(pltpu.with_memory_space_constraint(arg, pltpu.HBM))
        else:
            specs.append(pl.BlockSpec(memory_space=pltpu.VMEM))
            operands.append(pltpu.with_memory_space_constraint(arg, pltpu.VMEM))
    return pl.pallas_call(
        kernel,
        out_shape=out_shape,
        name=kernel.__name__,
        in_specs=specs,
        out_specs=jax.tree.map(lambda _: pl.BlockSpec(memory_space=out_space), out_shape),
        scratch_shapes=list(scratch),
        input_output_aliases=aliases or {},
        cost_estimate=pl.CostEstimate(
            flops=int(time * WEIGHT), transcendentals=0, bytes_accessed=int(time * 3.5e6)
        ),
        compiler_params=pltpu.CompilerParams(vmem_limit_bytes=VMEM_LIMIT),
    )(*operands)


def shape(dims, dtype):
    return jax.ShapeDtypeStruct(dims, dtype)


def kept(dims, dtype):
    return pltpu.VMEM(dims, dtype)


def pack_kernel(
    feat_hbm,
    filt_hbm,
    taps_hbm,
    grad_hbm,
    p0,
    p1,
    p2,
    p3,
    taps_out,
    feat_ref,
    filt_ref,
    taps_ref,
    grad_ref,
    held,
    square,
    sems,
):
    x = coords()[0]
    copies = []
    for place, (src, dst) in enumerate(
        (
            (feat_hbm, feat_ref),
            (filt_hbm, filt_ref),
            (taps_hbm, taps_ref),
            (grad_hbm, grad_ref),
        )
    ):
        copy = pltpu.make_async_copy(src, dst, sems.at[place])
        copy.start()
        copies.append(copy)
    square[0] = jnp.zeros((128, 256), F32)
    for copy in copies:
        copy.wait()
    for stream in range(4):
        flipped = (feat_ref[stream] if stream < 3 else filt_ref[...]).T
        for quarter in range(4):
            held[quarter, stream] = flipped[quarter * 64 : quarter * 64 + 64]
    for by, out in enumerate((p0, p1, p2, p3)):
        out[0:4] = held[lax.rem(x + by, 4)]
        for row in range(2):
            for column in range(2):
                out[4 + 2 * row + column] = grad_ref[
                    row * 64 : row * 64 + 64, column * 128 : column * 128 + 128
                ]
    for stream in range(3):
        square[0, stream * 8 : stream * 8 + TAPS, :] = taps_ref[stream]
    columns = square[0].T
    for quarter in range(4):
        square[1 + quarter, 0:64, 0:128] = columns[quarter * 64 : quarter * 64 + 64]
    taps_out[...] = square[1 + x, 0:64, 0:128]


def fetch_kernel(weight, high_hbm, low_hbm, behind, out, high, low, sems, table_sems):
    x, z, y, c = coords()
    copies = []
    for half in range(2):
        core = c if half == 0 else 1 - c
        for yd in range(NY):
            copies.append(
                pltpu.make_async_copy(
                    weight.at[:, yd, core, x], out.at[half, yd], sems.at[half, yd]
                )
            )
    copies.append(pltpu.make_async_copy(high_hbm, high, table_sems.at[0]))
    copies.append(pltpu.make_async_copy(low_hbm, low, table_sems.at[1]))
    for copy in copies:
        copy.start()
    for copy in copies:
        copy.wait()


def lift_kernel(p0, r1, r2, r3, rows, whole_out, send_out, gathered):
    x = coords()[0]
    for by, block in enumerate((p0, r1, r2, r3)):
        slot = lax.rem(x + 4 - by, 4)
        for row in range(2):
            for column in range(2):
                gathered[
                    slot, row * 64 : row * 64 + 64, column * 128 : column * 128 + 128
                ] = block[4 + 2 * row + column]
    whole = gathered[...].reshape(512, 256)
    whole_out[...] = whole
    for yd in range(NY):
        part = lax.dot_general(
            rows[1, yd].reshape(256, 256), whole, NT, preferred_element_type=F32
        )
        send_out[yd] = part.astype(BF16).reshape(NZ, 64, 512)


def sum_core_kernel(recv, whole, rows, behind, own_out, s1, s2, s3):
    y = coords()[2]
    for by, out in enumerate((own_out, s1, s2, s3)):
        yd = lax.rem(y + by, 4)
        part = lax.dot_general(
            rows[0, yd].reshape(256, 256), whole[...], NT, preferred_element_type=F32
        )
        total = part.reshape(NZ, 64, 512) + recv[yd].astype(F32)
        out[...] = total.astype(out.dtype)


def sum_y_kernel(own, r1, r2, r3, own_out, s1, s2, s3):
    z = coords()[1]
    for by, out in enumerate((own_out, s1, s2, s3)):
        zd = lax.rem(z + by, 4)
        total = (
            own[zd] + r1[zd].astype(F32) + (r2[zd].astype(F32) + r3[zd].astype(F32))
        )
        out[...] = total.astype(out.dtype)


def later(values, by, lane):
    if by == 0:
        return values
    return jnp.where(lane >= by, pltpu.roll(values, by, 1), 0.0)


def sooner(values, by, lane):
    if by == 0:
        return values
    return jnp.where(lane < 512 - by, pltpu.roll(values, 512 - by, 1), 0.0)


def split(values):
    high = values.astype(BF16)
    return high, (values - high.astype(F32)).astype(BF16)


def forward(rows, high, low):
    return jnp.dot(rows, high[...], preferred_element_type=F32) + jnp.dot(
        rows, low[...], preferred_element_type=F32
    )


def backward(spectra, high, low):
    count = spectra.shape[0]
    big, small = split(spectra)
    first = lax.dot_general(
        jnp.concatenate([big, small], axis=0), high[...], NT, preferred_element_type=F32
    )
    second = lax.dot_general(big, low[...], NT, preferred_element_type=F32)
    return (first[:count] + first[count:] + second) * (1.0 / 512)


def pre_kernel(p0, r1, r2, r3, taps, high, low, behind, mixed_out, conv_out, long_out, spec_out, feat_out, held):
    x = coords()[0]
    for by, block in enumerate((p0, r1, r2, r3)):
        held[lax.rem(x + 4 - by, 4)] = block[0:4]
    lane = lax.broadcasted_iota(jnp.int32, (64, 512), 1)
    convs = []
    for stream in range(3):
        feats = jnp.concatenate([held[b, stream] for b in range(4)], axis=1)
        feat_out[stream] = feats
        wide = feats.astype(F32)
        total = taps[:, stream * 8 : stream * 8 + 1] * wide
        for tap in range(1, TAPS):
            column = stream * 8 + tap
            total = total + taps[:, column : column + 1] * later(wide, tap, lane)
        conv_out[stream] = total
        convs.append(total)
    gated = (convs[1] * convs[2]).astype(BF16)
    filt = jnp.concatenate([held[b, 3] for b in range(4)], axis=1)
    spec = forward(jnp.concatenate([gated, filt], axis=0), high, low)
    spec_out[...] = spec
    gr, gi = spec[:64, :512], spec[:64, 512:]
    hr, hi = spec[64:, :512], spec[64:, 512:]
    product = jnp.concatenate([gr * hr - gi * hi, gr * hi + gi * hr], axis=1)
    long = backward(product, high, low)
    long_out[...] = long
    mixed_out[...] = (convs[0] * long).astype(BF16)


def post_kernel(own, r1, r2, r3, conv, long, spec, feats, taps, high, low, o0, o1, o2, o3, held):
    x = coords()[0]
    lane = lax.broadcasted_iota(jnp.int32, (64, 512), 1)
    grad_mixed = own[...] + r1[...].astype(F32) + (r2[...].astype(F32) + r3[...].astype(F32))
    grad_long = (grad_mixed * conv[0]).astype(BF16)
    lspec = forward(grad_long, high, low)
    lr, li = lspec[:, :512], lspec[:, 512:]
    gr, gi = spec[:64, :512], spec[:64, 512:]
    hr, hi = spec[64:, :512], spec[64:, 512:]
    to_gated = jnp.concatenate([hr * lr + hi * li, hr * li - hi * lr], axis=1)
    to_filter = jnp.concatenate([gr * lr + gi * li, gr * li - gi * lr], axis=1)
    both = backward(jnp.concatenate([to_gated, to_filter], axis=0), high, low)
    grad_gated, grad_filter = both[:64], both[64:]
    grad_conv = (grad_mixed * long[...], grad_gated * conv[2], grad_gated * conv[1])
    slot = lax.broadcasted_iota(jnp.int32, (64, 128), 1)
    sums = jnp.zeros((64, 128), F32)
    for stream in range(3):
        wide = feats[stream].astype(F32)
        total = None
        for tap in range(TAPS):
            column = stream * 8 + tap
            ahead = sooner(grad_conv[stream], tap, lane)
            term = taps[:, column : column + 1] * ahead
            total = term if total is None else total + term
            row = jnp.sum(ahead * wide, axis=1, keepdims=True)
            sums = jnp.where(slot == column, row, sums)
        rounded = total.astype(BF16)
        for b in range(4):
            held[b, stream] = rounded[:, b * 128 : b * 128 + 128]
    high_part, low_part = split(grad_filter)
    sums_high, sums_low = split(sums)
    sums_both = sums_high.astype(F32) + pltpu.roll(sums_low.astype(F32), 32, 1)
    for b in range(4):
        held[b, 3] = high_part[:, b * 128 : b * 128 + 128]
        held[b, 4] = low_part[:, b * 128 : b * 128 + 128]
        held[b, 5] = sums_both.astype(BF16)
    for by, out in enumerate((o0, o1, o2, o3)):
        out[...] = held[lax.rem(x + by, 4)]


def out_kernel(o0, r1, r2, r3, feat_out, taps_out, filt_out, held):
    x = coords()[0]
    for by, block in enumerate((o0, r1, r2, r3)):
        held[lax.rem(x + 4 - by, 4)] = block[...]
    for stream in range(3):
        columns = jnp.concatenate([held[q, stream] for q in range(4)], axis=0)
        feat_out[stream] = columns.T
    filt = jnp.concatenate(
        [held[q, 3].astype(F32) + held[q, 4].astype(F32) for q in range(4)], axis=0
    )
    filt_out[...] = filt.T
    sums = jnp.concatenate([held[q, 5].astype(F32) for q in range(4)], axis=0)
    sums = sums + pltpu.roll(sums, 96, 1)
    rows = sums.T
    for stream in range(3):
        taps_out[stream] = rows[stream * 8 : stream * 8 + TAPS]


def gate_kernel(block, out):
    out[...] = block[0, 0:8, 0:128]


def pair_kernel(b0, b1, behind, out):
    out[0] = b0[...]
    out[1] = b1[...]


def route_kernel(near, far, o0, o1, o2, o3, held):
    x, z = coords()[:2]
    for back in range(4):
        held[lax.rem(z + 4 - back, 4)] = (near if back < 2 else far)[back % 2]
    for by, out in enumerate((o0, o1, o2, o3)):
        out[...] = held[lax.rem(x + by, 4)]


def collect_kernel(b0, b1, b2, b3, out):
    for place, block in enumerate((b0, b1, b2, b3)):
        out[place] = block[...]


def weight_half(blocks, whole, out, parts, sems, core):
    x, z, y, c = coords()
    stores = []
    for along in range(4):
        yd = lax.rem(y + 4 - along, 4)
        part = jnp.dot(
            blocks[along].reshape(256, 512), whole[...], preferred_element_type=F32
        )
        for across in range(4):
            src = lax.rem(x + 4 - across, 4)
            parts[along, src] = part[across * 64 : across * 64 + 64]
        store = pltpu.make_async_copy(parts.at[along], out.at[yd, core], sems.at[along])
        store.start()
        stores.append(store)
    for store in stores:
        store.wait()


def near_kernel(blocks, whole, out, parts, sems):
    weight_half(blocks, whole, out, parts, sems, coords()[3])


def far_kernel(blocks, whole, held, out, parts, sems):
    weight_half(blocks, whole, out, parts, sems, 1 - coords()[3])


def local(high, low, features, short_kernel, long_filter, out_weight, grad_out):
    high, low = jnp.asarray(high), jnp.asarray(low)
    weight = out_weight.reshape(NZ, NY, NC, NX, 64, 256)
    *pay, taps = call(
        pack_kernel,
        [kept((8, 64, 128), BF16)] * 4 + [kept((64, 128), F32)],
        features,
        long_filter,
        short_kernel,
        grad_out,
        in_hbm=(0, 1, 2, 3),
        scratch=[
            pltpu.VMEM((3, 128, 256), BF16),
            pltpu.VMEM((128, 256), BF16),
            pltpu.VMEM((3, TAPS, 256), F32),
            pltpu.VMEM((128, 256), BF16),
            pltpu.VMEM((4, 4, 64, 128), BF16),
            pltpu.VMEM((5, 128, 256), F32),
            pltpu.SemaphoreType.DMA((4,)),
        ],
        time=TIMES["pack"],
    )
    got = [pay[0]] + [along_x(pay[k], k) for k in (1, 2, 3)]
    rows, high, low = call(
        fetch_kernel,
        [kept((2, NY, NZ, 64, 256), BF16)] + [kept((512, 1024), BF16)] * 2,
        weight,
        high,
        low,
        taps,
        in_hbm=(0, 1, 2),
        scratch=[pltpu.SemaphoreType.DMA((2, NY)), pltpu.SemaphoreType.DMA((2,))],
        time=TIMES["fetch"],
    )
    whole, send = call(
        lift_kernel,
        [kept((512, 256), BF16), kept((NY, NZ, 64, 512), BF16)],
        *got,
        rows,
        scratch=[pltpu.VMEM((4, 128, 256), BF16)],
        time=TIMES["lift"],
    )
    recv = other_core(send)
    mixed, conv, long, spec, feats = call(
        pre_kernel,
        [
            kept((64, 512), BF16),
            kept((3, 64, 512), F32),
            kept((64, 512), F32),
            kept((128, 1024), F32),
            kept((3, 64, 512), BF16),
        ],
        *got,
        taps,
        high,
        low,
        whole,
        scratch=[pltpu.VMEM((4, 4, 64, 128), BF16)],
        time=TIMES["pre"],
    )
    own, *sends = call(
        sum_core_kernel,
        [kept((NZ, 64, 512), F32)] + [kept((NZ, 64, 512), BF16)] * 3,
        recv,
        whole,
        rows,
        mixed,
        time=TIMES["core"],
    )
    recvs = [along_y(sends[k - 1], k) for k in (1, 2, 3)]
    gate = call(gate_kernel, kept((8, 128), BF16), sends[2], time=TIMES["gate"])
    pair = call(
        pair_kernel,
        kept((2, 64, 512), BF16),
        mixed,
        along_z(mixed, 1),
        gate,
        time=TIMES["pair"],
    )
    routed = call(
        route_kernel,
        [kept((64, 512), BF16)] * 4,
        pair,
        along_z(pair, 2),
        scratch=[pltpu.VMEM((4, 64, 512), BF16)],
        time=TIMES["relay"],
    )
    column = call(
        collect_kernel,
        kept((4, 64, 512), BF16),
        routed[0],
        *[along_x(routed[k], k) for k in (1, 2, 3)],
        time=TIMES["collect"],
    )
    mine = call(
        collect_kernel,
        kept((4, 4, 64, 512), BF16),
        column,
        *[along_y(column, k) for k in (1, 2, 3)],
        time=TIMES["collect"],
    )
    theirs = other_core(mine)
    own, *sends = call(
        sum_y_kernel,
        [kept((64, 512), F32)] + [kept((64, 512), BF16)] * 3,
        own,
        *recvs,
        time=TIMES["sum"],
    )
    recvs = [along_z(sends[k - 1], k) for k in (1, 2, 3)]
    outs = call(
        post_kernel,
        [kept((6, 64, 128), BF16)] * 4,
        own,
        *recvs,
        conv,
        long,
        spec,
        feats,
        taps,
        high,
        low,
        scratch=[pltpu.VMEM((4, 6, 64, 128), BF16)],
        time=TIMES["post"],
    )
    backs = [outs[0]] + [along_x(outs[k], k) for k in (1, 2, 3)]
    grad_features, grad_kernel, grad_filter = call(
        out_kernel,
        [shape((3, 128, 256), BF16), shape((3, TAPS, 256), F32), shape((128, 256), F32)],
        *backs,
        scratch=[pltpu.VMEM((4, 6, 64, 128), BF16)],
        time=TIMES["out"],
    )
    space = [pltpu.VMEM((NY, 4, 64, 256), F32), pltpu.SemaphoreType.DMA((NY,))]
    grad_weight = call(
        near_kernel,
        pltpu.HBM((NY, NC, 4, 64, 256), F32),
        mine,
        whole,
        out_hbm=True,
        scratch=space,
        time=TIMES["near"],
    )
    grad_weight = call(
        far_kernel,
        shape((NY, NC, 4, 64, 256), F32),
        theirs,
        whole,
        grad_weight,
        in_hbm=(2,),
        out_hbm=True,
        aliases={2: 0},
        scratch=space,
        time=TIMES["weight"],
    ).reshape(2048, 256)
    return grad_features, grad_kernel, grad_filter, grad_weight


def solution(mesh):
    high, low = wave_table(512)
    return jax.shard_map(
        functools.partial(local, high, low),
        mesh=mesh,
        in_specs=(
            P(None, "ctx", "ch"),
            P(None, None, "ch"),
            P("ctx", "ch"),
            P(None, "ch"),
            P("ctx", "ch"),
        ),
        out_specs=(P(None, "ctx", "ch"), P(None, None, "ch"), P("ctx", "ch"), P("ctx", "ch")),
        check_vma=False,
    )
```

```python
import functools
import math

import jax
import jax.numpy as jnp
import numpy as np
from jax import lax
from jax.experimental import pallas as pl
from jax.experimental.pallas import tpu as pltpu
from jax.sharding import PartitionSpec as P

F32 = jnp.float32
BF16 = jnp.bfloat16
NX, NZ, NY, NC = 4, 4, 4, 2
TAPS = 7
NT = (((1,), (1,)), ((), ()))
VMEM_LIMIT = 20 * 1024 * 1024
WEIGHT = 3.5e10
TIMES = dict(
    pack=2, fetch=2, lift=2, core=2, pre=2, relay=0, collect=0, sum=0.3, post=3, out=1, weight=2, near=0, pair=0, gate=0.3
)


def coords():
    x = lax.axis_index("ctx")
    ch = lax.axis_index("ch")
    return x, ch // 8, lax.rem(ch // 2, 4), lax.rem(ch, 2)


def flat(x, z, y, c):
    return ((x * NZ + z) * NY + y) * NC + c


def move(array, rule):
    pairs = []
    for x in range(NX):
        for z in range(NZ):
            for y in range(NY):
                for c in range(NC):
                    pairs.append((flat(x, z, y, c), flat(*rule(x, z, y, c))))
    return lax.ppermute(array, ("ctx", "ch"), pairs)


def along_x(array, by):
    return move(array, lambda x, z, y, c: ((x + by) % NX, z, y, c))


def along_z(array, by):
    return move(array, lambda x, z, y, c: (x, (z + by) % NZ, y, c))


def along_y(array, by):
    return move(array, lambda x, z, y, c: (x, z, (y + by) % NY, c))


def other_core(array):
    return move(array, lambda x, z, y, c: (x, z, y, 1 - c))


def wave_table(length):
    period = 2 * length
    freq = 2 * np.arange(length) + 1
    steps = np.arange(length)
    angle = (steps[:, None] * freq[None, :] % (2 * period)) * (math.pi / period)
    table = np.concatenate([np.cos(angle), -np.sin(angle)], axis=1)
    high = table.astype(jnp.bfloat16)
    low = (table - high.astype(np.float64)).astype(jnp.bfloat16)
    return high, low


def call(
    kernel, out_shape, *args, scratch=(), in_hbm=(), out_hbm=False, aliases=None, time=2.0
):
    out_space = pl.ANY if out_hbm else pltpu.VMEM
    specs, operands = [], []
    for place, arg in enumerate(args):
        if place in in_hbm:
            specs.append(pl.BlockSpec(memory_space=pl.ANY))
            operands.append(pltpu.with_memory_space_constraint(arg, pltpu.HBM))
        else:
            specs.append(pl.BlockSpec(memory_space=pltpu.VMEM))
            operands.append(pltpu.with_memory_space_constraint(arg, pltpu.VMEM))
    return pl.pallas_call(
        kernel,
        out_shape=out_shape,
        name=kernel.__name__,
        in_specs=specs,
        out_specs=jax.tree.map(lambda _: pl.BlockSpec(memory_space=out_space), out_shape),
        scratch_shapes=list(scratch),
        input_output_aliases=aliases or {},
        cost_estimate=pl.CostEstimate(
            flops=int(time * WEIGHT), transcendentals=0, bytes_accessed=int(time * 3.5e6)
        ),
        compiler_params=pltpu.CompilerParams(vmem_limit_bytes=VMEM_LIMIT),
    )(*operands)


def shape(dims, dtype):
    return jax.ShapeDtypeStruct(dims, dtype)


def kept(dims, dtype):
    return pltpu.VMEM(dims, dtype)


def pack_kernel(
    feat_hbm,
    filt_hbm,
    taps_hbm,
    grad_hbm,
    p0,
    p1,
    p2,
    p3,
    taps_out,
    feat_ref,
    filt_ref,
    taps_ref,
    grad_ref,
    held,
    square,
    sems,
):
    x = coords()[0]
    copies = []
    for place, (src, dst) in enumerate(
        (
            (feat_hbm, feat_ref),
            (filt_hbm, filt_ref),
            (taps_hbm, taps_ref),
            (grad_hbm, grad_ref),
        )
    ):
        copy = pltpu.make_async_copy(src, dst, sems.at[place])
        copy.start()
        copies.append(copy)
    square[0] = jnp.zeros((128, 256), F32)
    for copy in copies:
        copy.wait()
    for stream in range(4):
        flipped = (feat_ref[stream] if stream < 3 else filt_ref[...]).T
        for quarter in range(4):
            held[quarter, stream] = flipped[quarter * 64 : quarter * 64 + 64]
    for by, out in enumerate((p0, p1, p2, p3)):
        out[0:4] = held[lax.rem(x + by, 4)]
        for row in range(2):
            for column in range(2):
                out[4 + 2 * row + column] = grad_ref[
                    row * 64 : row * 64 + 64, column * 128 : column * 128 + 128
                ]
    for stream in range(3):
        square[0, stream * 8 : stream * 8 + TAPS, :] = taps_ref[stream]
    columns = square[0].T
    for quarter in range(4):
        square[1 + quarter, 0:64, 0:128] = columns[quarter * 64 : quarter * 64 + 64]
    taps_out[...] = square[1 + x, 0:64, 0:128]


def fetch_kernel(weight, high_hbm, low_hbm, behind, out, high, low, sems, table_sems):
    x, z, y, c = coords()
    copies = []
    for half in range(2):
        core = c if half == 0 else 1 - c
        for yd in range(NY):
            copies.append(
                pltpu.make_async_copy(
                    weight.at[:, yd, core, x], out.at[half, yd], sems.at[half, yd]
                )
            )
    copies.append(pltpu.make_async_copy(high_hbm, high, table_sems.at[0]))
    copies.append(pltpu.make_async_copy(low_hbm, low, table_sems.at[1]))
    for copy in copies:
        copy.start()
    for copy in copies:
        copy.wait()


def lift_kernel(p0, r1, r2, r3, rows, whole_out, send_out, gathered):
    x = coords()[0]
    for by, block in enumerate((p0, r1, r2, r3)):
        slot = lax.rem(x + 4 - by, 4)
        for row in range(2):
            for column in range(2):
                gathered[
                    slot, row * 64 : row * 64 + 64, column * 128 : column * 128 + 128
                ] = block[4 + 2 * row + column]
    whole = gathered[...].reshape(512, 256)
    whole_out[...] = whole
    for yd in range(NY):
        part = lax.dot_general(
            rows[1, yd].reshape(256, 256), whole, NT, preferred_element_type=F32
        )
        send_out[yd] = part.astype(BF16).reshape(NZ, 64, 512)


def sum_core_kernel(recv, whole, rows, behind, own_out, s1, s2, s3):
    y = coords()[2]
    for by, out in enumerate((own_out, s1, s2, s3)):
        yd = lax.rem(y + by, 4)
        part = lax.dot_general(
            rows[0, yd].reshape(256, 256), whole[...], NT, preferred_element_type=F32
        )
        total = part.reshape(NZ, 64, 512) + recv[yd].astype(F32)
        out[...] = total.astype(out.dtype)


def sum_y_kernel(own, r1, r2, r3, own_out, s1, s2, s3):
    z = coords()[1]
    for by, out in enumerate((own_out, s1, s2, s3)):
        zd = lax.rem(z + by, 4)
        total = (
            own[zd] + r1[zd].astype(F32) + (r2[zd].astype(F32) + r3[zd].astype(F32))
        )
        out[...] = total.astype(out.dtype)


def later(values, by, lane):
    if by == 0:
        return values
    return jnp.where(lane >= by, pltpu.roll(values, by, 1), 0.0)


def sooner(values, by, lane):
    if by == 0:
        return values
    return jnp.where(lane < 512 - by, pltpu.roll(values, 512 - by, 1), 0.0)


def split(values):
    high = values.astype(BF16)
    return high, (values - high.astype(F32)).astype(BF16)


def forward(rows, high, low):
    return jnp.dot(rows, high[...], preferred_element_type=F32) + jnp.dot(
        rows, low[...], preferred_element_type=F32
    )


def backward(spectra, high, low):
    count = spectra.shape[0]
    big, small = split(spectra)
    first = lax.dot_general(
        jnp.concatenate([big, small], axis=0), high[...], NT, preferred_element_type=F32
    )
    second = lax.dot_general(big, low[...], NT, preferred_element_type=F32)
    return (first[:count] + first[count:] + second) * (1.0 / 512)


def pre_kernel(p0, r1, r2, r3, taps, high, low, behind, mixed_out, conv_out, long_out, spec_out, feat_out, held):
    x = coords()[0]
    for by, block in enumerate((p0, r1, r2, r3)):
        held[lax.rem(x + 4 - by, 4)] = block[0:4]
    lane = lax.broadcasted_iota(jnp.int32, (64, 512), 1)
    convs = []
    for stream in range(3):
        feats = jnp.concatenate([held[b, stream] for b in range(4)], axis=1)
        feat_out[stream] = feats
        wide = feats.astype(F32)
        total = taps[:, stream * 8 : stream * 8 + 1] * wide
        for tap in range(1, TAPS):
            column = stream * 8 + tap
            total = total + taps[:, column : column + 1] * later(wide, tap, lane)
        conv_out[stream] = total
        convs.append(total)
    gated = (convs[1] * convs[2]).astype(BF16)
    filt = jnp.concatenate([held[b, 3] for b in range(4)], axis=1)
    spec = forward(jnp.concatenate([gated, filt], axis=0), high, low)
    spec_out[...] = spec
    gr, gi = spec[:64, :512], spec[:64, 512:]
    hr, hi = spec[64:, :512], spec[64:, 512:]
    product = jnp.concatenate([gr * hr - gi * hi, gr * hi + gi * hr], axis=1)
    long = backward(product, high, low)
    long_out[...] = long
    mixed_out[...] = (convs[0] * long).astype(BF16)


def post_kernel(own, r1, r2, r3, conv, long, spec, feats, taps, high, low, o0, o1, o2, o3, held):
    x = coords()[0]
    lane = lax.broadcasted_iota(jnp.int32, (64, 512), 1)
    grad_mixed = own[...] + r1[...].astype(F32) + (r2[...].astype(F32) + r3[...].astype(F32))
    grad_long = (grad_mixed * conv[0]).astype(BF16)
    lspec = forward(grad_long, high, low)
    lr, li = lspec[:, :512], lspec[:, 512:]
    gr, gi = spec[:64, :512], spec[:64, 512:]
    hr, hi = spec[64:, :512], spec[64:, 512:]
    to_gated = jnp.concatenate([hr * lr + hi * li, hr * li - hi * lr], axis=1)
    to_filter = jnp.concatenate([gr * lr + gi * li, gr * li - gi * lr], axis=1)
    both = backward(jnp.concatenate([to_gated, to_filter], axis=0), high, low)
    grad_gated, grad_filter = both[:64], both[64:]
    grad_conv = (grad_mixed * long[...], grad_gated * conv[2], grad_gated * conv[1])
    slot = lax.broadcasted_iota(jnp.int32, (64, 128), 1)
    sums = jnp.zeros((64, 128), F32)
    for stream in range(3):
        wide = feats[stream].astype(F32)
        total = None
        for tap in range(TAPS):
            column = stream * 8 + tap
            ahead = sooner(grad_conv[stream], tap, lane)
            term = taps[:, column : column + 1] * ahead
            total = term if total is None else total + term
            row = jnp.sum(ahead * wide, axis=1, keepdims=True)
            sums = jnp.where(slot == column, row, sums)
        rounded = total.astype(BF16)
        for b in range(4):
            held[b, stream] = rounded[:, b * 128 : b * 128 + 128]
    high_part, low_part = split(grad_filter)
    sums_high, sums_low = split(sums)
    sums_both = sums_high.astype(F32) + pltpu.roll(sums_low.astype(F32), 32, 1)
    for b in range(4):
        held[b, 3] = high_part[:, b * 128 : b * 128 + 128]
        held[b, 4] = low_part[:, b * 128 : b * 128 + 128]
        held[b, 5] = sums_both.astype(BF16)
    for by, out in enumerate((o0, o1, o2, o3)):
        out[...] = held[lax.rem(x + by, 4)]


def out_kernel(o0, r1, r2, r3, feat_out, taps_out, filt_out, held):
    x = coords()[0]
    for by, block in enumerate((o0, r1, r2, r3)):
        held[lax.rem(x + 4 - by, 4)] = block[...]
    for stream in range(3):
        columns = jnp.concatenate([held[q, stream] for q in range(4)], axis=0)
        feat_out[stream] = columns.T
    filt = jnp.concatenate(
        [held[q, 3].astype(F32) + held[q, 4].astype(F32) for q in range(4)], axis=0
    )
    filt_out[...] = filt.T
    sums = jnp.concatenate([held[q, 5].astype(F32) for q in range(4)], axis=0)
    sums = sums + pltpu.roll(sums, 96, 1)
    rows = sums.T
    for stream in range(3):
        taps_out[stream] = rows[stream * 8 : stream * 8 + TAPS]


def gate_kernel(block, out):
    out[...] = block[0, 0:8, 0:128]


def pair_kernel(b0, b1, behind, out):
    out[0] = b0[...]
    out[1] = b1[...]


def route_kernel(near, far, o0, o1, o2, o3, held):
    x, z = coords()[:2]
    for back in range(4):
        held[lax.rem(z + 4 - back, 4)] = (far if back % 2 else near)[back // 2]
    for by, out in enumerate((o0, o1, o2, o3)):
        out[...] = held[lax.rem(x + by, 4)]


def collect_kernel(b0, b1, b2, b3, out):
    for place, block in enumerate((b0, b1, b2, b3)):
        out[place] = block[...]


def weight_half(blocks, whole, out, parts, sems, core):
    x, z, y, c = coords()
    stores = []
    for along in range(4):
        yd = lax.rem(y + 4 - along, 4)
        part = jnp.dot(
            blocks[along].reshape(256, 512), whole[...], preferred_element_type=F32
        )
        for across in range(4):
            src = lax.rem(x + 4 - across, 4)
            parts[along, src] = part[across * 64 : across * 64 + 64]
        store = pltpu.make_async_copy(parts.at[along], out.at[yd, core], sems.at[along])
        store.start()
        stores.append(store)
    for store in stores:
        store.wait()


def near_kernel(blocks, whole, out, parts, sems):
    weight_half(blocks, whole, out, parts, sems, coords()[3])


def far_kernel(blocks, whole, held, out, parts, sems):
    weight_half(blocks, whole, out, parts, sems, 1 - coords()[3])


def local(high, low, features, short_kernel, long_filter, out_weight, grad_out):
    high, low = jnp.asarray(high), jnp.asarray(low)
    weight = out_weight.reshape(NZ, NY, NC, NX, 64, 256)
    *pay, taps = call(
        pack_kernel,
        [kept((8, 64, 128), BF16)] * 4 + [kept((64, 128), F32)],
        features,
        long_filter,
        short_kernel,
        grad_out,
        in_hbm=(0, 1, 2, 3),
        scratch=[
            pltpu.VMEM((3, 128, 256), BF16),
            pltpu.VMEM((128, 256), BF16),
            pltpu.VMEM((3, TAPS, 256), F32),
            pltpu.VMEM((128, 256), BF16),
            pltpu.VMEM((4, 4, 64, 128), BF16),
            pltpu.VMEM((5, 128, 256), F32),
            pltpu.SemaphoreType.DMA((4,)),
        ],
        time=TIMES["pack"],
    )
    got = [pay[0]] + [along_x(pay[k], k) for k in (1, 2, 3)]
    rows, high, low = call(
        fetch_kernel,
        [kept((2, NY, NZ, 64, 256), BF16)] + [kept((512, 1024), BF16)] * 2,
        weight,
        high,
        low,
        taps,
        in_hbm=(0, 1, 2),
        scratch=[pltpu.SemaphoreType.DMA((2, NY)), pltpu.SemaphoreType.DMA((2,))],
        time=TIMES["fetch"],
    )
    whole, send = call(
        lift_kernel,
        [kept((512, 256), BF16), kept((NY, NZ, 64, 512), BF16)],
        *got,
        rows,
        scratch=[pltpu.VMEM((4, 128, 256), BF16)],
        time=TIMES["lift"],
    )
    recv = other_core(send)
    mixed, conv, long, spec, feats = call(
        pre_kernel,
        [
            kept((64, 512), BF16),
            kept((3, 64, 512), F32),
            kept((64, 512), F32),
            kept((128, 1024), F32),
            kept((3, 64, 512), BF16),
        ],
        *got,
        taps,
        high,
        low,
        whole,
        scratch=[pltpu.VMEM((4, 4, 64, 128), BF16)],
        time=TIMES["pre"],
    )
    own, *sends = call(
        sum_core_kernel,
        [kept((NZ, 64, 512), F32)] + [kept((NZ, 64, 512), BF16)] * 3,
        recv,
        whole,
        rows,
        mixed,
        time=TIMES["core"],
    )
    recvs = [along_y(sends[k - 1], k) for k in (1, 2, 3)]
    gate = call(gate_kernel, kept((8, 128), BF16), sends[2], time=TIMES["gate"])
    pair = call(
        pair_kernel,
        kept((2, 64, 512), BF16),
        mixed,
        along_z(mixed, 2),
        gate,
        time=TIMES["pair"],
    )
    routed = call(
        route_kernel,
        [kept((64, 512), BF16)] * 4,
        pair,
        along_z(pair, 1),
        scratch=[pltpu.VMEM((4, 64, 512), BF16)],
        time=TIMES["relay"],
    )
    column = call(
        collect_kernel,
        kept((4, 64, 512), BF16),
        routed[0],
        *[along_x(routed[k], k) for k in (1, 2, 3)],
        time=TIMES["collect"],
    )
    mine = call(
        collect_kernel,
        kept((4, 4, 64, 512), BF16),
        column,
        *[along_y(column, k) for k in (1, 2, 3)],
        time=TIMES["collect"],
    )
    theirs = other_core(mine)
    own, *sends = call(
        sum_y_kernel,
        [kept((64, 512), F32)] + [kept((64, 512), BF16)] * 3,
        own,
        *recvs,
        time=TIMES["sum"],
    )
    recvs = [along_z(sends[k - 1], k) for k in (1, 2, 3)]
    outs = call(
        post_kernel,
        [kept((6, 64, 128), BF16)] * 4,
        own,
        *recvs,
        conv,
        long,
        spec,
        feats,
        taps,
        high,
        low,
        scratch=[pltpu.VMEM((4, 6, 64, 128), BF16)],
        time=TIMES["post"],
    )
    backs = [outs[0]] + [along_x(outs[k], k) for k in (1, 2, 3)]
    grad_features, grad_kernel, grad_filter = call(
        out_kernel,
        [shape((3, 128, 256), BF16), shape((3, TAPS, 256), F32), shape((128, 256), F32)],
        *backs,
        scratch=[pltpu.VMEM((4, 6, 64, 128), BF16)],
        time=TIMES["out"],
    )
    space = [pltpu.VMEM((NY, 4, 64, 256), F32), pltpu.SemaphoreType.DMA((NY,))]
    grad_weight = call(
        near_kernel,
        pltpu.HBM((NY, NC, 4, 64, 256), F32),
        mine,
        whole,
        out_hbm=True,
        scratch=space,
        time=TIMES["near"],
    )
    grad_weight = call(
        far_kernel,
        shape((NY, NC, 4, 64, 256), F32),
        theirs,
        whole,
        grad_weight,
        in_hbm=(2,),
        out_hbm=True,
        aliases={2: 0},
        scratch=space,
        time=TIMES["weight"],
    ).reshape(2048, 256)
    return grad_features, grad_kernel, grad_filter, grad_weight


def solution(mesh):
    high, low = wave_table(512)
    return jax.shard_map(
        functools.partial(local, high, low),
        mesh=mesh,
        in_specs=(
            P(None, "ctx", "ch"),
            P(None, None, "ch"),
            P("ctx", "ch"),
            P(None, "ch"),
            P("ctx", "ch"),
        ),
        out_specs=(P(None, "ctx", "ch"), P(None, None, "ch"), P("ctx", "ch"), P("ctx", "ch")),
        check_vma=False,
    )
```

```python
import functools
import math

import jax
import jax.numpy as jnp
import numpy as np
from jax import lax
from jax.experimental import pallas as pl
from jax.experimental.pallas import tpu as pltpu
from jax.sharding import PartitionSpec as P

F32 = jnp.float32
BF16 = jnp.bfloat16
NX, NZ, NY, NC = 4, 4, 4, 2
TAPS = 7
NT = (((1,), (1,)), ((), ()))
VMEM_LIMIT = 20 * 1024 * 1024
WEIGHT = 3.5e10
TIMES = dict(
    pack=2, fetch=2, lift=2, core=2, pre=2, relay=0, collect=0, sum=0.3, post=3, out=1, weight=2, near=0, pair=0, gate=0.3
)


def coords():
    x = lax.axis_index("ctx")
    ch = lax.axis_index("ch")
    return x, ch // 8, lax.rem(ch // 2, 4), lax.rem(ch, 2)


def flat(x, z, y, c):
    return ((x * NZ + z) * NY + y) * NC + c


def move(array, rule):
    pairs = []
    for x in range(NX):
        for z in range(NZ):
            for y in range(NY):
                for c in range(NC):
                    pairs.append((flat(x, z, y, c), flat(*rule(x, z, y, c))))
    return lax.ppermute(array, ("ctx", "ch"), pairs)


def along_x(array, by):
    return move(array, lambda x, z, y, c: ((x + by) % NX, z, y, c))


def along_z(array, by):
    return move(array, lambda x, z, y, c: (x, (z + by) % NZ, y, c))


def along_y(array, by):
    return move(array, lambda x, z, y, c: (x, z, (y + by) % NY, c))


def other_core(array):
    return move(array, lambda x, z, y, c: (x, z, y, 1 - c))


def wave_table(length):
    period = 2 * length
    freq = 2 * np.arange(length) + 1
    steps = np.arange(length)
    angle = (steps[:, None] * freq[None, :] % (2 * period)) * (math.pi / period)
    table = np.concatenate([np.cos(angle), -np.sin(angle)], axis=1)
    high = table.astype(jnp.bfloat16)
    low = (table - high.astype(np.float64)).astype(jnp.bfloat16)
    return high, low


def call(
    kernel, out_shape, *args, scratch=(), in_hbm=(), out_hbm=False, aliases=None, time=2.0
):
    out_space = pl.ANY if out_hbm else pltpu.VMEM
    specs, operands = [], []
    for place, arg in enumerate(args):
        if place in in_hbm:
            specs.append(pl.BlockSpec(memory_space=pl.ANY))
            operands.append(pltpu.with_memory_space_constraint(arg, pltpu.HBM))
        else:
            specs.append(pl.BlockSpec(memory_space=pltpu.VMEM))
            operands.append(pltpu.with_memory_space_constraint(arg, pltpu.VMEM))
    return pl.pallas_call(
        kernel,
        out_shape=out_shape,
        name=kernel.__name__,
        in_specs=specs,
        out_specs=jax.tree.map(lambda _: pl.BlockSpec(memory_space=out_space), out_shape),
        scratch_shapes=list(scratch),
        input_output_aliases=aliases or {},
        cost_estimate=pl.CostEstimate(
            flops=int(time * WEIGHT), transcendentals=0, bytes_accessed=int(time * 3.5e6)
        ),
        compiler_params=pltpu.CompilerParams(vmem_limit_bytes=VMEM_LIMIT),
    )(*operands)


def shape(dims, dtype):
    return jax.ShapeDtypeStruct(dims, dtype)


def kept(dims, dtype):
    return pltpu.VMEM(dims, dtype)


def pack_kernel(
    feat_hbm,
    filt_hbm,
    grad_hbm,
    p0,
    p1,
    p2,
    p3,
    feat_ref,
    filt_ref,
    grad_ref,
    held,
    sems,
):
    x = coords()[0]
    copies = []
    for place, (src, dst) in enumerate(
        (
            (feat_hbm, feat_ref),
            (filt_hbm, filt_ref),
            (grad_hbm, grad_ref),
        )
    ):
        copy = pltpu.make_async_copy(src, dst, sems.at[place])
        copy.start()
        copies.append(copy)
    for copy in copies:
        copy.wait()
    for stream in range(4):
        flipped = (feat_ref[stream] if stream < 3 else filt_ref[...]).T
        for quarter in range(4):
            held[quarter, stream] = flipped[quarter * 64 : quarter * 64 + 64]
    for by, out in enumerate((p0, p1, p2, p3)):
        out[0:4] = held[lax.rem(x + by, 4)]
        for row in range(2):
            for column in range(2):
                out[4 + 2 * row + column] = grad_ref[
                    row * 64 : row * 64 + 64, column * 128 : column * 128 + 128
                ]


def fetch_kernel(
    weight,
    high_hbm,
    low_hbm,
    taps_ref,
    behind,
    out,
    high,
    low,
    taps_out,
    square,
    sems,
    table_sems,
):
    x, z, y, c = coords()
    copies = []
    for half in range(2):
        core = c if half == 0 else 1 - c
        for yd in range(NY):
            copies.append(
                pltpu.make_async_copy(
                    weight.at[:, yd, core, x], out.at[half, yd], sems.at[half, yd]
                )
            )
    copies.append(pltpu.make_async_copy(high_hbm, high, table_sems.at[0]))
    copies.append(pltpu.make_async_copy(low_hbm, low, table_sems.at[1]))
    for copy in copies:
        copy.start()
    square[0] = jnp.zeros((128, 256), F32)
    for stream in range(3):
        square[0, stream * 8 : stream * 8 + TAPS, :] = taps_ref[stream]
    columns = square[0].T
    for quarter in range(4):
        square[1 + quarter, 0:64, 0:128] = columns[quarter * 64 : quarter * 64 + 64]
    taps_out[...] = square[1 + x, 0:64, 0:128]
    for copy in copies:
        copy.wait()


def lift_kernel(p0, r1, r2, r3, rows, whole_out, send_out, gathered):
    x = coords()[0]
    for by, block in enumerate((p0, r1, r2, r3)):
        slot = lax.rem(x + 4 - by, 4)
        for row in range(2):
            for column in range(2):
                gathered[
                    slot, row * 64 : row * 64 + 64, column * 128 : column * 128 + 128
                ] = block[4 + 2 * row + column]
    whole = gathered[...].reshape(512, 256)
    whole_out[...] = whole
    for yd in range(NY):
        part = lax.dot_general(
            rows[1, yd].reshape(256, 256), whole, NT, preferred_element_type=F32
        )
        send_out[yd] = part.astype(BF16).reshape(NZ, 64, 512)


def sum_core_kernel(recv, whole, rows, behind, own_out, s1, s2, s3):
    y = coords()[2]
    for by, out in enumerate((own_out, s1, s2, s3)):
        yd = lax.rem(y + by, 4)
        part = lax.dot_general(
            rows[0, yd].reshape(256, 256), whole[...], NT, preferred_element_type=F32
        )
        total = part.reshape(NZ, 64, 512) + recv[yd].astype(F32)
        out[...] = total.astype(out.dtype)


def sum_y_kernel(own, r1, r2, r3, own_out, s1, s2, s3):
    z = coords()[1]
    for by, out in enumerate((own_out, s1, s2, s3)):
        zd = lax.rem(z + by, 4)
        total = (
            own[zd] + r1[zd].astype(F32) + (r2[zd].astype(F32) + r3[zd].astype(F32))
        )
        out[...] = total.astype(out.dtype)


def later(values, by, lane):
    if by == 0:
        return values
    return jnp.where(lane >= by, pltpu.roll(values, by, 1), 0.0)


def sooner(values, by, lane):
    if by == 0:
        return values
    return jnp.where(lane < 512 - by, pltpu.roll(values, 512 - by, 1), 0.0)


def split(values):
    high = values.astype(BF16)
    return high, (values - high.astype(F32)).astype(BF16)


def forward(rows, high, low):
    return jnp.dot(rows, high[...], preferred_element_type=F32) + jnp.dot(
        rows, low[...], preferred_element_type=F32
    )


def backward(spectra, high, low):
    count = spectra.shape[0]
    big, small = split(spectra)
    first = lax.dot_general(
        jnp.concatenate([big, small], axis=0), high[...], NT, preferred_element_type=F32
    )
    second = lax.dot_general(big, low[...], NT, preferred_element_type=F32)
    return (first[:count] + first[count:] + second) * (1.0 / 512)


def pre_kernel(p0, r1, r2, r3, taps, high, low, behind, mixed_out, conv_out, long_out, spec_out, feat_out, held):
    x = coords()[0]
    for by, block in enumerate((p0, r1, r2, r3)):
        held[lax.rem(x + 4 - by, 4)] = block[0:4]
    lane = lax.broadcasted_iota(jnp.int32, (64, 512), 1)
    convs = []
    for stream in range(3):
        feats = jnp.concatenate([held[b, stream] for b in range(4)], axis=1)
        feat_out[stream] = feats
        wide = feats.astype(F32)
        total = taps[:, stream * 8 : stream * 8 + 1] * wide
        for tap in range(1, TAPS):
            column = stream * 8 + tap
            total = total + taps[:, column : column + 1] * later(wide, tap, lane)
        conv_out[stream] = total
        convs.append(total)
    gated = (convs[1] * convs[2]).astype(BF16)
    filt = jnp.concatenate([held[b, 3] for b in range(4)], axis=1)
    spec = forward(jnp.concatenate([gated, filt], axis=0), high, low)
    spec_out[...] = spec
    gr, gi = spec[:64, :512], spec[:64, 512:]
    hr, hi = spec[64:, :512], spec[64:, 512:]
    product = jnp.concatenate([gr * hr - gi * hi, gr * hi + gi * hr], axis=1)
    long = backward(product, high, low)
    long_out[...] = long
    mixed_out[...] = (convs[0] * long).astype(BF16)


def post_kernel(own, r1, r2, r3, conv, long, spec, feats, taps, high, low, o0, o1, o2, o3, held):
    x = coords()[0]
    lane = lax.broadcasted_iota(jnp.int32, (64, 512), 1)
    grad_mixed = own[...] + r1[...].astype(F32) + (r2[...].astype(F32) + r3[...].astype(F32))
    grad_long = (grad_mixed * conv[0]).astype(BF16)
    lspec = forward(grad_long, high, low)
    lr, li = lspec[:, :512], lspec[:, 512:]
    gr, gi = spec[:64, :512], spec[:64, 512:]
    hr, hi = spec[64:, :512], spec[64:, 512:]
    to_gated = jnp.concatenate([hr * lr + hi * li, hr * li - hi * lr], axis=1)
    to_filter = jnp.concatenate([gr * lr + gi * li, gr * li - gi * lr], axis=1)
    both = backward(jnp.concatenate([to_gated, to_filter], axis=0), high, low)
    grad_gated, grad_filter = both[:64], both[64:]
    grad_conv = (grad_mixed * long[...], grad_gated * conv[2], grad_gated * conv[1])
    slot = lax.broadcasted_iota(jnp.int32, (64, 128), 1)
    sums = jnp.zeros((64, 128), F32)
    for stream in range(3):
        wide = feats[stream].astype(F32)
        total = None
        for tap in range(TAPS):
            column = stream * 8 + tap
            ahead = sooner(grad_conv[stream], tap, lane)
            term = taps[:, column : column + 1] * ahead
            total = term if total is None else total + term
            row = jnp.sum(ahead * wide, axis=1, keepdims=True)
            sums = jnp.where(slot == column, row, sums)
        rounded = total.astype(BF16)
        for b in range(4):
            held[b, stream] = rounded[:, b * 128 : b * 128 + 128]
    high_part, low_part = split(grad_filter)
    sums_high, sums_low = split(sums)
    sums_both = sums_high.astype(F32) + pltpu.roll(sums_low.astype(F32), 32, 1)
    for b in range(4):
        held[b, 3] = high_part[:, b * 128 : b * 128 + 128]
        held[b, 4] = low_part[:, b * 128 : b * 128 + 128]
        held[b, 5] = sums_both.astype(BF16)
    for by, out in enumerate((o0, o1, o2, o3)):
        out[...] = held[lax.rem(x + by, 4)]


def out_kernel(o0, r1, r2, r3, feat_out, taps_out, filt_out, held):
    x = coords()[0]
    for by, block in enumerate((o0, r1, r2, r3)):
        held[lax.rem(x + 4 - by, 4)] = block[...]
    for stream in range(3):
        columns = jnp.concatenate([held[q, stream] for q in range(4)], axis=0)
        feat_out[stream] = columns.T
    filt = jnp.concatenate(
        [held[q, 3].astype(F32) + held[q, 4].astype(F32) for q in range(4)], axis=0
    )
    filt_out[...] = filt.T
    sums = jnp.concatenate([held[q, 5].astype(F32) for q in range(4)], axis=0)
    sums = sums + pltpu.roll(sums, 96, 1)
    rows = sums.T
    for stream in range(3):
        taps_out[stream] = rows[stream * 8 : stream * 8 + TAPS]


def gate_kernel(block, out):
    out[...] = block[0, 0:8, 0:128]


def pair_kernel(b0, b1, behind, out):
    out[0] = b0[...]
    out[1] = b1[...]


def route_kernel(near, far, o0, o1, o2, o3, held):
    x, z = coords()[:2]
    for back in range(4):
        held[lax.rem(z + 4 - back, 4)] = (far if back % 2 else near)[back // 2]
    for by, out in enumerate((o0, o1, o2, o3)):
        out[...] = held[lax.rem(x + by, 4)]


def collect_kernel(b0, b1, b2, b3, out):
    for place, block in enumerate((b0, b1, b2, b3)):
        out[place] = block[...]


def weight_half(blocks, whole, out, parts, sems, core):
    x, z, y, c = coords()
    stores = []
    for along in range(4):
        yd = lax.rem(y + 4 - along, 4)
        part = jnp.dot(
            blocks[along].reshape(256, 512), whole[...], preferred_element_type=F32
        )
        for across in range(4):
            src = lax.rem(x + 4 - across, 4)
            parts[along, src] = part[across * 64 : across * 64 + 64]
        store = pltpu.make_async_copy(parts.at[along], out.at[yd, core], sems.at[along])
        store.start()
        stores.append(store)
    for store in stores:
        store.wait()


def near_kernel(blocks, whole, out, parts, sems):
    weight_half(blocks, whole, out, parts, sems, coords()[3])


def far_kernel(blocks, whole, held, out, parts, sems):
    weight_half(blocks, whole, out, parts, sems, 1 - coords()[3])


def local(high, low, features, short_kernel, long_filter, out_weight, grad_out):
    high, low = jnp.asarray(high), jnp.asarray(low)
    weight = out_weight.reshape(NZ, NY, NC, NX, 64, 256)
    pay = call(
        pack_kernel,
        [kept((8, 64, 128), BF16)] * 4,
        features,
        long_filter,
        grad_out,
        in_hbm=(0, 1, 2),
        scratch=[
            pltpu.VMEM((3, 128, 256), BF16),
            pltpu.VMEM((128, 256), BF16),
            pltpu.VMEM((128, 256), BF16),
            pltpu.VMEM((4, 4, 64, 128), BF16),
            pltpu.SemaphoreType.DMA((3,)),
        ],
        time=TIMES["pack"],
    )
    got = [pay[0]] + [along_x(pay[k], k) for k in (1, 2, 3)]
    rows, high, low, taps = call(
        fetch_kernel,
        [kept((2, NY, NZ, 64, 256), BF16)]
        + [kept((512, 1024), BF16)] * 2
        + [kept((64, 128), F32)],
        weight,
        high,
        low,
        short_kernel,
        pay[0],
        in_hbm=(0, 1, 2),
        scratch=[pltpu.VMEM((5, 128, 256), F32), pltpu.SemaphoreType.DMA((2, NY)), pltpu.SemaphoreType.DMA((2,))],
        time=TIMES["fetch"],
    )
    whole, send = call(
        lift_kernel,
        [kept((512, 256), BF16), kept((NY, NZ, 64, 512), BF16)],
        *got,
        rows,
        scratch=[pltpu.VMEM((4, 128, 256), BF16)],
        time=TIMES["lift"],
    )
    recv = other_core(send)
    mixed, conv, long, spec, feats = call(
        pre_kernel,
        [
            kept((64, 512), BF16),
            kept((3, 64, 512), F32),
            kept((64, 512), F32),
            kept((128, 1024), F32),
            kept((3, 64, 512), BF16),
        ],
        *got,
        taps,
        high,
        low,
        whole,
        scratch=[pltpu.VMEM((4, 4, 64, 128), BF16)],
        time=TIMES["pre"],
    )
    own, *sends = call(
        sum_core_kernel,
        [kept((NZ, 64, 512), F32)] + [kept((NZ, 64, 512), BF16)] * 3,
        recv,
        whole,
        rows,
        mixed,
        time=TIMES["core"],
    )
    recvs = [along_y(sends[k - 1], k) for k in (1, 2, 3)]
    gate = call(gate_kernel, kept((8, 128), BF16), sends[2], time=TIMES["gate"])
    pair = call(
        pair_kernel,
        kept((2, 64, 512), BF16),
        mixed,
        along_z(mixed, 2),
        gate,
        time=TIMES["pair"],
    )
    routed = call(
        route_kernel,
        [kept((64, 512), BF16)] * 4,
        pair,
        along_z(pair, 1),
        scratch=[pltpu.VMEM((4, 64, 512), BF16)],
        time=TIMES["relay"],
    )
    column = call(
        collect_kernel,
        kept((4, 64, 512), BF16),
        routed[0],
        *[along_x(routed[k], k) for k in (1, 2, 3)],
        time=TIMES["collect"],
    )
    mine = call(
        collect_kernel,
        kept((4, 4, 64, 512), BF16),
        column,
        *[along_y(column, k) for k in (1, 2, 3)],
        time=TIMES["collect"],
    )
    theirs = other_core(mine)
    own, *sends = call(
        sum_y_kernel,
        [kept((64, 512), F32)] + [kept((64, 512), BF16)] * 3,
        own,
        *recvs,
        time=TIMES["sum"],
    )
    recvs = [along_z(sends[k - 1], k) for k in (1, 2, 3)]
    outs = call(
        post_kernel,
        [kept((6, 64, 128), BF16)] * 4,
        own,
        *recvs,
        conv,
        long,
        spec,
        feats,
        taps,
        high,
        low,
        scratch=[pltpu.VMEM((4, 6, 64, 128), BF16)],
        time=TIMES["post"],
    )
    backs = [outs[0]] + [along_x(outs[k], k) for k in (1, 2, 3)]
    grad_features, grad_kernel, grad_filter = call(
        out_kernel,
        [shape((3, 128, 256), BF16), shape((3, TAPS, 256), F32), shape((128, 256), F32)],
        *backs,
        scratch=[pltpu.VMEM((4, 6, 64, 128), BF16)],
        time=TIMES["out"],
    )
    space = [pltpu.VMEM((NY, 4, 64, 256), F32), pltpu.SemaphoreType.DMA((NY,))]
    grad_weight = call(
        near_kernel,
        pltpu.HBM((NY, NC, 4, 64, 256), F32),
        mine,
        whole,
        out_hbm=True,
        scratch=space,
        time=TIMES["near"],
    )
    grad_weight = call(
        far_kernel,
        shape((NY, NC, 4, 64, 256), F32),
        theirs,
        whole,
        grad_weight,
        in_hbm=(2,),
        out_hbm=True,
        aliases={2: 0},
        scratch=space,
        time=TIMES["weight"],
    ).reshape(2048, 256)
    return grad_features, grad_kernel, grad_filter, grad_weight


def solution(mesh):
    high, low = wave_table(512)
    return jax.shard_map(
        functools.partial(local, high, low),
        mesh=mesh,
        in_specs=(
            P(None, "ctx", "ch"),
            P(None, None, "ch"),
            P("ctx", "ch"),
            P(None, "ch"),
            P("ctx", "ch"),
        ),
        out_specs=(P(None, "ctx", "ch"), P(None, None, "ch"), P("ctx", "ch"), P("ctx", "ch")),
        check_vma=False,
    )
```

```python
import functools
import math

import jax
import jax.numpy as jnp
import numpy as np
from jax import lax
from jax.experimental import pallas as pl
from jax.experimental.pallas import tpu as pltpu
from jax.sharding import PartitionSpec as P

F32 = jnp.float32
BF16 = jnp.bfloat16
NX, NZ, NY, NC = 4, 4, 4, 2
TAPS = 7
NT = (((1,), (1,)), ((), ()))
VMEM_LIMIT = 20 * 1024 * 1024
WEIGHT = 3.5e10
TIMES = dict(
    pack=2, fetch=2, lift=2, core=2, pre=2, relay=0, collect=0, sum=0.3, post=3, out=1, weight=2, near=0, pair=0, gate=0.3
)


def coords():
    x = lax.axis_index("ctx")
    ch = lax.axis_index("ch")
    return x, ch // 8, lax.rem(ch // 2, 4), lax.rem(ch, 2)


def flat(x, z, y, c):
    return ((x * NZ + z) * NY + y) * NC + c


def move(array, rule):
    pairs = []
    for x in range(NX):
        for z in range(NZ):
            for y in range(NY):
                for c in range(NC):
                    pairs.append((flat(x, z, y, c), flat(*rule(x, z, y, c))))
    return lax.ppermute(array, ("ctx", "ch"), pairs)


def along_x(array, by):
    return move(array, lambda x, z, y, c: ((x + by) % NX, z, y, c))


def along_z(array, by):
    return move(array, lambda x, z, y, c: (x, (z + by) % NZ, y, c))


def along_y(array, by):
    return move(array, lambda x, z, y, c: (x, z, (y + by) % NY, c))


def other_core(array):
    return move(array, lambda x, z, y, c: (x, z, y, 1 - c))


def wave_table(length):
    period = 2 * length
    freq = 2 * np.arange(length) + 1
    steps = np.arange(length)
    angle = (steps[:, None] * freq[None, :] % (2 * period)) * (math.pi / period)
    table = np.concatenate([np.cos(angle), -np.sin(angle)], axis=1)
    high = table.astype(jnp.bfloat16)
    low = (table - high.astype(np.float64)).astype(jnp.bfloat16)
    return high, low


def call(
    kernel, out_shape, *args, scratch=(), in_hbm=(), out_hbm=False, aliases=None, time=2.0
):
    out_space = pl.ANY if out_hbm else pltpu.VMEM
    specs, operands = [], []
    for place, arg in enumerate(args):
        if place in in_hbm:
            specs.append(pl.BlockSpec(memory_space=pl.ANY))
            operands.append(pltpu.with_memory_space_constraint(arg, pltpu.HBM))
        else:
            specs.append(pl.BlockSpec(memory_space=pltpu.VMEM))
            operands.append(pltpu.with_memory_space_constraint(arg, pltpu.VMEM))
    return pl.pallas_call(
        kernel,
        out_shape=out_shape,
        name=kernel.__name__,
        in_specs=specs,
        out_specs=jax.tree.map(lambda _: pl.BlockSpec(memory_space=out_space), out_shape),
        scratch_shapes=list(scratch),
        input_output_aliases=aliases or {},
        cost_estimate=pl.CostEstimate(
            flops=int(time * WEIGHT), transcendentals=0, bytes_accessed=int(time * 3.5e6)
        ),
        compiler_params=pltpu.CompilerParams(vmem_limit_bytes=VMEM_LIMIT),
    )(*operands)


def shape(dims, dtype):
    return jax.ShapeDtypeStruct(dims, dtype)


def kept(dims, dtype):
    return pltpu.VMEM(dims, dtype)


def pack_kernel(
    feat_hbm,
    filt_hbm,
    grad_hbm,
    p0,
    p1,
    p2,
    p3,
    feat_ref,
    filt_ref,
    grad_ref,
    held,
    sems,
):
    x = coords()[0]
    copies = []
    for place, (src, dst) in enumerate(
        (
            (feat_hbm, feat_ref),
            (filt_hbm, filt_ref),
            (grad_hbm, grad_ref),
        )
    ):
        copy = pltpu.make_async_copy(src, dst, sems.at[place])
        copy.start()
        copies.append(copy)
    copies[0].wait()
    for stream in range(4):
        if stream == 3:
            copies[1].wait()
        flipped = (feat_ref[stream] if stream < 3 else filt_ref[...]).T
        for quarter in range(4):
            held[quarter, stream] = flipped[quarter * 64 : quarter * 64 + 64]
    copies[2].wait()
    for by, out in enumerate((p0, p1, p2, p3)):
        out[0:4] = held[lax.rem(x + by, 4)]
        for row in range(2):
            for column in range(2):
                out[4 + 2 * row + column] = grad_ref[
                    row * 64 : row * 64 + 64, column * 128 : column * 128 + 128
                ]


def fetch_kernel(
    weight,
    high_hbm,
    low_hbm,
    taps_ref,
    behind,
    out,
    high,
    low,
    taps_out,
    square,
    sems,
    table_sems,
):
    x, z, y, c = coords()
    copies = []
    for half in range(2):
        core = c if half == 0 else 1 - c
        for yd in range(NY):
            copies.append(
                pltpu.make_async_copy(
                    weight.at[:, yd, core, x], out.at[half, yd], sems.at[half, yd]
                )
            )
    copies.append(pltpu.make_async_copy(high_hbm, high, table_sems.at[0]))
    copies.append(pltpu.make_async_copy(low_hbm, low, table_sems.at[1]))
    for copy in copies:
        copy.start()
    square[0] = jnp.zeros((128, 256), F32)
    for stream in range(3):
        square[0, stream * 8 : stream * 8 + TAPS, :] = taps_ref[stream]
    columns = square[0].T
    for quarter in range(4):
        square[1 + quarter, 0:64, 0:128] = columns[quarter * 64 : quarter * 64 + 64]
    taps_out[...] = square[1 + x, 0:64, 0:128]
    for copy in copies:
        copy.wait()


def lift_kernel(p0, r1, r2, r3, rows, whole_out, send_out, gathered):
    x = coords()[0]
    for by, block in enumerate((p0, r1, r2, r3)):
        slot = lax.rem(x + 4 - by, 4)
        for row in range(2):
            for column in range(2):
                gathered[
                    slot, row * 64 : row * 64 + 64, column * 128 : column * 128 + 128
                ] = block[4 + 2 * row + column]
    whole = gathered[...].reshape(512, 256)
    whole_out[...] = whole
    for yd in range(NY):
        part = lax.dot_general(
            rows[1, yd].reshape(256, 256), whole, NT, preferred_element_type=F32
        )
        send_out[yd] = part.astype(BF16).reshape(NZ, 64, 512)


def sum_core_kernel(recv, whole, rows, behind, own_out, s1, s2, s3):
    y = coords()[2]
    for by, out in enumerate((own_out, s1, s2, s3)):
        yd = lax.rem(y + by, 4)
        part = lax.dot_general(
            rows[0, yd].reshape(256, 256), whole[...], NT, preferred_element_type=F32
        )
        total = part.reshape(NZ, 64, 512) + recv[yd].astype(F32)
        out[...] = total.astype(out.dtype)


def sum_y_kernel(own, r1, r2, r3, own_out, s1, s2, s3):
    z = coords()[1]
    for by, out in enumerate((own_out, s1, s2, s3)):
        zd = lax.rem(z + by, 4)
        total = (
            own[zd] + r1[zd].astype(F32) + (r2[zd].astype(F32) + r3[zd].astype(F32))
        )
        out[...] = total.astype(out.dtype)


def later(values, by, lane):
    if by == 0:
        return values
    return jnp.where(lane >= by, pltpu.roll(values, by, 1), 0.0)


def sooner(values, by, lane):
    if by == 0:
        return values
    return jnp.where(lane < 512 - by, pltpu.roll(values, 512 - by, 1), 0.0)


def split(values):
    high = values.astype(BF16)
    return high, (values - high.astype(F32)).astype(BF16)


def forward(rows, high, low):
    return jnp.dot(rows, high[...], preferred_element_type=F32) + jnp.dot(
        rows, low[...], preferred_element_type=F32
    )


def backward(spectra, high, low):
    count = spectra.shape[0]
    big, small = split(spectra)
    first = lax.dot_general(
        jnp.concatenate([big, small], axis=0), high[...], NT, preferred_element_type=F32
    )
    second = lax.dot_general(big, low[...], NT, preferred_element_type=F32)
    return (first[:count] + first[count:] + second) * (1.0 / 512)


def pre_kernel(p0, r1, r2, r3, taps, high, low, behind, mixed_out, conv_out, long_out, spec_out, feat_out, held):
    x = coords()[0]
    for by, block in enumerate((p0, r1, r2, r3)):
        held[lax.rem(x + 4 - by, 4)] = block[0:4]
    lane = lax.broadcasted_iota(jnp.int32, (64, 512), 1)
    convs = []
    for stream in range(3):
        feats = jnp.concatenate([held[b, stream] for b in range(4)], axis=1)
        feat_out[stream] = feats
        wide = feats.astype(F32)
        total = taps[:, stream * 8 : stream * 8 + 1] * wide
        for tap in range(1, TAPS):
            column = stream * 8 + tap
            total = total + taps[:, column : column + 1] * later(wide, tap, lane)
        conv_out[stream] = total
        convs.append(total)
    gated = (convs[1] * convs[2]).astype(BF16)
    filt = jnp.concatenate([held[b, 3] for b in range(4)], axis=1)
    spec = forward(jnp.concatenate([gated, filt], axis=0), high, low)
    spec_out[...] = spec
    gr, gi = spec[:64, :512], spec[:64, 512:]
    hr, hi = spec[64:, :512], spec[64:, 512:]
    product = jnp.concatenate([gr * hr - gi * hi, gr * hi + gi * hr], axis=1)
    long = backward(product, high, low)
    long_out[...] = long
    mixed_out[...] = (convs[0] * long).astype(BF16)


def post_kernel(own, r1, r2, r3, conv, long, spec, feats, taps, high, low, o0, o1, o2, o3, held):
    x = coords()[0]
    lane = lax.broadcasted_iota(jnp.int32, (64, 512), 1)
    grad_mixed = own[...] + r1[...].astype(F32) + (r2[...].astype(F32) + r3[...].astype(F32))
    grad_long = (grad_mixed * conv[0]).astype(BF16)
    lspec = forward(grad_long, high, low)
    lr, li = lspec[:, :512], lspec[:, 512:]
    gr, gi = spec[:64, :512], spec[:64, 512:]
    hr, hi = spec[64:, :512], spec[64:, 512:]
    to_gated = jnp.concatenate([hr * lr + hi * li, hr * li - hi * lr], axis=1)
    to_filter = jnp.concatenate([gr * lr + gi * li, gr * li - gi * lr], axis=1)
    both = backward(jnp.concatenate([to_gated, to_filter], axis=0), high, low)
    grad_gated, grad_filter = both[:64], both[64:]
    grad_conv = (grad_mixed * long[...], grad_gated * conv[2], grad_gated * conv[1])
    slot = lax.broadcasted_iota(jnp.int32, (64, 128), 1)
    sums = jnp.zeros((64, 128), F32)
    for stream in range(3):
        wide = feats[stream].astype(F32)
        total = None
        for tap in range(TAPS):
            column = stream * 8 + tap
            ahead = sooner(grad_conv[stream], tap, lane)
            term = taps[:, column : column + 1] * ahead
            total = term if total is None else total + term
            row = jnp.sum(ahead * wide, axis=1, keepdims=True)
            sums = jnp.where(slot == column, row, sums)
        rounded = total.astype(BF16)
        for b in range(4):
            held[b, stream] = rounded[:, b * 128 : b * 128 + 128]
    high_part, low_part = split(grad_filter)
    sums_high, sums_low = split(sums)
    sums_both = sums_high.astype(F32) + pltpu.roll(sums_low.astype(F32), 32, 1)
    for b in range(4):
        held[b, 3] = high_part[:, b * 128 : b * 128 + 128]
        held[b, 4] = low_part[:, b * 128 : b * 128 + 128]
        held[b, 5] = sums_both.astype(BF16)
    for by, out in enumerate((o0, o1, o2, o3)):
        out[...] = held[lax.rem(x + by, 4)]


def out_kernel(o0, r1, r2, r3, feat_out, taps_out, filt_out, held):
    x = coords()[0]
    for by, block in enumerate((o0, r1, r2, r3)):
        held[lax.rem(x + 4 - by, 4)] = block[...]
    for stream in range(3):
        columns = jnp.concatenate([held[q, stream] for q in range(4)], axis=0)
        feat_out[stream] = columns.T
    filt = jnp.concatenate(
        [held[q, 3].astype(F32) + held[q, 4].astype(F32) for q in range(4)], axis=0
    )
    filt_out[...] = filt.T
    sums = jnp.concatenate([held[q, 5].astype(F32) for q in range(4)], axis=0)
    sums = sums + pltpu.roll(sums, 96, 1)
    rows = sums.T
    for stream in range(3):
        taps_out[stream] = rows[stream * 8 : stream * 8 + TAPS]


def gate_kernel(block, out):
    out[...] = block[0, 0:8, 0:128]


def pair_kernel(b0, b1, behind, out):
    out[0] = b0[...]
    out[1] = b1[...]


def route_kernel(near, far, o0, o1, o2, o3, held):
    x, z = coords()[:2]
    for back in range(4):
        held[lax.rem(z + 4 - back, 4)] = (far if back % 2 else near)[back // 2]
    for by, out in enumerate((o0, o1, o2, o3)):
        out[...] = held[lax.rem(x + by, 4)]


def collect_kernel(b0, b1, b2, b3, out):
    for place, block in enumerate((b0, b1, b2, b3)):
        out[place] = block[...]


def weight_half(blocks, whole, out, parts, sems, core):
    x, z, y, c = coords()
    stores = []
    for along in range(4):
        yd = lax.rem(y + 4 - along, 4)
        part = jnp.dot(
            blocks[along].reshape(256, 512), whole[...], preferred_element_type=F32
        )
        for across in range(4):
            src = lax.rem(x + 4 - across, 4)
            parts[along, src] = part[across * 64 : across * 64 + 64]
        store = pltpu.make_async_copy(parts.at[along], out.at[yd, core], sems.at[along])
        store.start()
        stores.append(store)
    for store in stores:
        store.wait()


def near_kernel(blocks, whole, out, parts, sems):
    weight_half(blocks, whole, out, parts, sems, coords()[3])


def far_kernel(blocks, whole, held, out, parts, sems):
    weight_half(blocks, whole, out, parts, sems, 1 - coords()[3])


def local(high, low, features, short_kernel, long_filter, out_weight, grad_out):
    high, low = jnp.asarray(high), jnp.asarray(low)
    weight = out_weight.reshape(NZ, NY, NC, NX, 64, 256)
    pay = call(
        pack_kernel,
        [kept((8, 64, 128), BF16)] * 4,
        features,
        long_filter,
        grad_out,
        in_hbm=(0, 1, 2),
        scratch=[
            pltpu.VMEM((3, 128, 256), BF16),
            pltpu.VMEM((128, 256), BF16),
            pltpu.VMEM((128, 256), BF16),
            pltpu.VMEM((4, 4, 64, 128), BF16),
            pltpu.SemaphoreType.DMA((3,)),
        ],
        time=TIMES["pack"],
    )
    got = [pay[0]] + [along_x(pay[k], k) for k in (1, 2, 3)]
    rows, high, low, taps = call(
        fetch_kernel,
        [kept((2, NY, NZ, 64, 256), BF16)]
        + [kept((512, 1024), BF16)] * 2
        + [kept((64, 128), F32)],
        weight,
        high,
        low,
        short_kernel,
        pay[0],
        in_hbm=(0, 1, 2),
        scratch=[pltpu.VMEM((5, 128, 256), F32), pltpu.SemaphoreType.DMA((2, NY)), pltpu.SemaphoreType.DMA((2,))],
        time=TIMES["fetch"],
    )
    whole, send = call(
        lift_kernel,
        [kept((512, 256), BF16), kept((NY, NZ, 64, 512), BF16)],
        *got,
        rows,
        scratch=[pltpu.VMEM((4, 128, 256), BF16)],
        time=TIMES["lift"],
    )
    recv = other_core(send)
    mixed, conv, long, spec, feats = call(
        pre_kernel,
        [
            kept((64, 512), BF16),
            kept((3, 64, 512), F32),
            kept((64, 512), F32),
            kept((128, 1024), F32),
            kept((3, 64, 512), BF16),
        ],
        *got,
        taps,
        high,
        low,
        whole,
        scratch=[pltpu.VMEM((4, 4, 64, 128), BF16)],
        time=TIMES["pre"],
    )
    own, *sends = call(
        sum_core_kernel,
        [kept((NZ, 64, 512), F32)] + [kept((NZ, 64, 512), BF16)] * 3,
        recv,
        whole,
        rows,
        mixed,
        time=TIMES["core"],
    )
    recvs = [along_y(sends[k - 1], k) for k in (1, 2, 3)]
    gate = call(gate_kernel, kept((8, 128), BF16), sends[2], time=TIMES["gate"])
    pair = call(
        pair_kernel,
        kept((2, 64, 512), BF16),
        mixed,
        along_z(mixed, 2),
        gate,
        time=TIMES["pair"],
    )
    routed = call(
        route_kernel,
        [kept((64, 512), BF16)] * 4,
        pair,
        along_z(pair, 1),
        scratch=[pltpu.VMEM((4, 64, 512), BF16)],
        time=TIMES["relay"],
    )
    column = call(
        collect_kernel,
        kept((4, 64, 512), BF16),
        routed[0],
        *[along_x(routed[k], k) for k in (1, 2, 3)],
        time=TIMES["collect"],
    )
    mine = call(
        collect_kernel,
        kept((4, 4, 64, 512), BF16),
        column,
        *[along_y(column, k) for k in (1, 2, 3)],
        time=TIMES["collect"],
    )
    theirs = other_core(mine)
    own, *sends = call(
        sum_y_kernel,
        [kept((64, 512), F32)] + [kept((64, 512), BF16)] * 3,
        own,
        *recvs,
        time=TIMES["sum"],
    )
    recvs = [along_z(sends[k - 1], k) for k in (1, 2, 3)]
    outs = call(
        post_kernel,
        [kept((6, 64, 128), BF16)] * 4,
        own,
        *recvs,
        conv,
        long,
        spec,
        feats,
        taps,
        high,
        low,
        scratch=[pltpu.VMEM((4, 6, 64, 128), BF16)],
        time=TIMES["post"],
    )
    backs = [outs[0]] + [along_x(outs[k], k) for k in (1, 2, 3)]
    grad_features, grad_kernel, grad_filter = call(
        out_kernel,
        [shape((3, 128, 256), BF16), shape((3, TAPS, 256), F32), shape((128, 256), F32)],
        *backs,
        scratch=[pltpu.VMEM((4, 6, 64, 128), BF16)],
        time=TIMES["out"],
    )
    space = [pltpu.VMEM((NY, 4, 64, 256), F32), pltpu.SemaphoreType.DMA((NY,))]
    grad_weight = call(
        near_kernel,
        pltpu.HBM((NY, NC, 4, 64, 256), F32),
        mine,
        whole,
        out_hbm=True,
        scratch=space,
        time=TIMES["near"],
    )
    grad_weight = call(
        far_kernel,
        shape((NY, NC, 4, 64, 256), F32),
        theirs,
        whole,
        grad_weight,
        in_hbm=(2,),
        out_hbm=True,
        aliases={2: 0},
        scratch=space,
        time=TIMES["weight"],
    ).reshape(2048, 256)
    return grad_features, grad_kernel, grad_filter, grad_weight


def solution(mesh):
    high, low = wave_table(512)
    return jax.shard_map(
        functools.partial(local, high, low),
        mesh=mesh,
        in_specs=(
            P(None, "ctx", "ch"),
            P(None, None, "ch"),
            P("ctx", "ch"),
            P(None, "ch"),
            P("ctx", "ch"),
        ),
        out_specs=(P(None, "ctx", "ch"), P(None, None, "ch"), P("ctx", "ch"), P("ctx", "ch")),
        check_vma=False,
    )
```
